128 devices in a mesh: cuts: 8 (over x_lo, z), dom: 16 (over y, x_hi, core).
Axes of the slice: x: 4 (x_hi: 2, x_lo: 2; x = x_hi * 2 + x_lo), y: 4, z: 4, core: 2. Of those that a mesh axis runs over, the one named last changes fastest.
Arguments:
- radiation: float32 [256, 16, 512], P('dom', 'cuts'), may hold values from -6 to 6
- electrons: float32 [2, 16, 32768], P(None, 'cuts', 'dom'), may hold values from -6 to 6
- cell_index: int32 [2, 16, 32768], P(None, 'cuts', 'dom'), may hold values from 0 to 254
- cell_offset: float32 [2, 16, 32768], P(None, 'cuts', 'dom'), may hold values from 0 to 1
- kernel_x: float32 [2, 256, 256], replicated, may hold values from -0.25 to 0.25
- kernel_y: float32 [2, 256, 256], replicated, may hold values from -0.25 to 0.25
Outputs:
- radiation_out: float32 [256, 16, 512], P('dom', 'cuts')
- electrons_out: float32 [2, 16, 32768], P(None, 'cuts', 'dom')
The draws below stay inside these ranges and needn't reach their ends.
Inputs may be any that keep to these rules, and one draw needn't show every extreme that they name: `cell_index`: the field is interpolated between cell and cell + 1 in each dimension, so every index stays below 255.
All inputs are finite; a program needn't handle non-finite values.
Results may differ from the reference program's by a relative error of at most 0.0003.
Values sent between devices are 32-bit elements; how exact they have to be, the bound alone decides.
A program may use at most 64 MiB of HBM per device.

```python
import jax
import jax.numpy as jnp
from jax import lax

G = 256
ITERS = 4
SLICES = 16
ELEC = 32768


def plant(entries, rng, smallest, largest):
    longest = entries.shape.index(max(entries.shape))
    spots = []
    for shift in (0, 1):
        where = [jax.random.randint(jax.random.fold_in(rng, axis), (), 0, length) for axis, length in enumerate(entries.shape)]
        where[longest] = (where[longest] + shift) % entries.shape[longest]
        spots.append(tuple(where))
    return entries.at[spots[0]].set(smallest).at[spots[1]].set(largest)


def shard_levels(rng, dims, pieces, low, largest):
    def one(dim, blocks):
        draws = jax.random.uniform(jax.random.fold_in(jax.random.fold_in(rng, 6), dim), (blocks,), jnp.float32, low / len(pieces), largest / len(pieces))
        return jnp.repeat(jnp.exp(draws), dims[dim] // blocks).reshape((-1,) + (1,) * (len(dims) - dim - 1))

    gain = one(*pieces[0])
    for cut in pieces[1:]:
        gain = gain * one(*cut)
    return gain


def noise(stream_key, shape, scale, limit, shards=(), kind=jnp.bfloat16):
    drawn = jax.random.normal(stream_key, shape, jnp.float32) * scale
    if len(shards) > 0:
        drawn = shard_levels(stream_key, shape, shards, -0.22, 0.18) * drawn
    return jnp.clip(drawn, min=-limit, max=limit).astype(kind)


def setup_inputs(seed: int = 0) -> dict:
    keys = jax.random.split(jax.random.key(seed), 7)
    radiation = noise(keys[0], (G, SLICES, 2 * G), 1.0, 6.0, ((0, 16), (1, 8)), jnp.float32)
    electrons = noise(keys[1], (2, SLICES, ELEC), 1.5, 6.0, ((1, 8), (2, 16)), jnp.float32)
    cell_index = plant(jax.random.randint(keys[2], (2, SLICES, ELEC), 0, G - 1), jax.random.fold_in(keys[2], 1), 0, (G - 1) - 1).astype(jnp.int32)
    cell_offset = jnp.clip(1.0 * jax.random.uniform(keys[3], (2, SLICES, ELEC), jnp.float32) ** shard_levels(keys[3], (2, SLICES, ELEC), ((1, 8), (2, 16)), -0.2, 0.2), 0.0, 1.0)
    kernel_x = noise(keys[4], (2, G, G), (2 * G) ** -0.5, 0.25, (), jnp.float32)
    kernel_y = noise(keys[5], (2, G, G), (2 * G) ** -0.5, 0.25, (), jnp.float32)
    return {"radiation": radiation, "electrons": electrons, "cell_index": cell_index, "cell_offset": cell_offset, "kernel_x": kernel_x, "kernel_y": kernel_y}


coupling = 0.5
phase_step = 1.0
current_gain = 1.0
highest = lax.Precision.HIGHEST


def tent_weights(index, offset):
    grid = jnp.arange(G, dtype=jnp.int32)
    lower = jnp.where(grid[None, :] == index[:, None], 1.0 - offset[:, None], 0.0)
    upper = jnp.where(grid[None, :] == index[:, None] + 1, offset[:, None], 0.0)
    return lower + upper


def one_slice(packed):
    field_s, phase, energy, row_idx, col_idx, row_off, col_off = packed
    weight_x = tent_weights(row_idx, row_off)
    weight_y = tent_weights(col_idx, col_off)
    projected = jnp.dot(weight_x, field_s, precision=highest)
    field_real = jnp.sum(projected[:, :G] * weight_y, axis=1)
    field_imag = jnp.sum(projected[:, G:] * weight_y, axis=1)
    energy = energy - coupling * (field_real * jnp.cos(phase) - field_imag * jnp.sin(phase))
    phase = phase + phase_step * energy
    values = jnp.concatenate([weight_y * jnp.cos(phase)[:, None], -weight_y * jnp.sin(phase)[:, None]], axis=1)
    current = jnp.dot(weight_x.T, values, precision=highest)
    return field_s + current_gain * current, phase, energy


def reference(radiation, electrons, cell_index, cell_offset, kernel_x, kernel_y):
    fields = jnp.transpose(radiation, (1, 0, 2))
    phases = electrons[0]
    energies = electrons[1]
    top = jnp.concatenate([kernel_y[0], kernel_y[1]], axis=1)
    bottom = jnp.concatenate([-kernel_y[1], kernel_y[0]], axis=1)
    big_y = jnp.concatenate([top, bottom], axis=0)
    for number in range(ITERS):
        updated, phases, energies = lax.map(one_slice, (fields, phases, energies, cell_index[0], cell_index[1], cell_offset[0], cell_offset[1]))
        left_re = jnp.einsum("ij,sjc->sic", kernel_x[0], updated, precision=highest)
        left_im = jnp.einsum("ij,sjc->sic", kernel_x[1], updated, precision=highest)
        real_part = left_re[:, :, :G] - left_im[:, :, G:]
        imag_part = left_re[:, :, G:] + left_im[:, :, :G]
        mixed = jnp.concatenate([real_part, imag_part], axis=2)
        mixed = jnp.einsum("sic,cd->sid", mixed, big_y, precision=highest)
        fields = jnp.concatenate([jnp.zeros_like(mixed[:1]), mixed[:-1]], axis=0)
    return jnp.transpose(fields, (1, 0, 2)), jnp.stack([phases, energies])
```

```python
import jax
import jax.numpy as jnp
from jax import lax
from jax.experimental import pallas as pl
from jax.experimental.pallas import tpu as pltpu
from jax.sharding import PartitionSpec as P

ITERS = 4
SLICES = 16
coupling = 0.5
phase_step = 1.0
current_gain = 1.0
MESH = pl.DeviceIdType.MESH
f32 = jnp.float32
bf16 = jnp.bfloat16

BLOCKS = 4
ROWS = 8
LANES = 256


def split(value):
    hi = value.astype(bf16)
    return hi, (value - hi.astype(f32)).astype(bf16)


def mm(a, b):
    return jnp.dot(a, b, preferred_element_type=f32)


def mm_nt(a, b):
    return lax.dot_general(a, b, (((1,), (1,)), ((), ())), preferred_element_type=f32)


def role_device(number, y, core):
    pair = number // 2
    x_hi, z = pair // 4, pair % 4
    x_lo = (number % 2 + z + x_hi) % 2
    return x_lo * 4 + z, y * 4 + x_hi * 2 + core


def home_device(number, x_hi, y, core):
    return number // 2, y * 4 + x_hi * 2 + core


def kernel(
    rad,
    el_in,
    kx,
    ky,
    rad_out,
    el_out,
    el,
    wx,
    wy,
    field,
    shift,
    a_send,
    a_recv,
    trig,
    v_hi,
    v_lo,
    current,
    k2,
    big_y,
    mixed,
    sums,
    p_send,
    p_out,
    el_send,
    init_send,
    el_sem,
    row_send,
    row_sem,
    ag_send,
    ag_sem,
    a_ssem,
    a_rsem,
    rs_send,
    rs_sem,
    sh_send,
    sh_sem,
    out_send,
    out_sem,
):
    cuts, dom = lax.axis_index("cuts"), lax.axis_index("dom")
    x_lo, z = cuts // 4, cuts % 4
    y, x_hi, core = dom // 4, dom // 2 % 2, dom % 2
    number = 2 * (x_hi * 4 + z) + (x_lo + z + x_hi) % 2
    q = y * 2 + core
    following = (number + 1) % SLICES

    def remote(src, dst, ssem, rsem, device):
        return pltpu.make_async_remote_copy(
            src_ref=src,
            dst_ref=dst,
            send_sem=ssem,
            recv_sem=rsem,
            device_id=device,
            device_id_type=MESH,
        )

    def send(src, dst, ssem, rsem, device):
        self_target = jnp.logical_and(device[0] == cuts, device[1] == dom)

        @pl.when(self_target)
        def _():
            pltpu.make_async_copy(src, dst, rsem).start()

        @pl.when(jnp.logical_not(self_target))
        def _():
            remote(src, dst, ssem, rsem, device).start()

    def sent(src, dst, ssem, rsem, device):
        self_target = jnp.logical_and(device[0] == cuts, device[1] == dom)

        @pl.when(jnp.logical_not(self_target))
        def _():
            remote(src, dst, ssem, rsem, device).wait_send()

    def received(dst, rsem):
        pltpu.make_async_copy(dst, dst, rsem).wait()

    own_slot = x_hi * 2 + core
    starts = []
    for p in range(2):
        target = role_device(2 * cuts + p, y, core)
        other = role_device(2 * cuts + p, y, 1 - core)
        starts.append(
            (el_in.at[p], el.at[own_slot], init_send.at[p, 0], el_sem.at[own_slot], target)
        )
        starts.append(
            (el_in.at[p], el.at[own_slot], init_send.at[p, 1], el_sem.at[own_slot], other)
        )
        starts.append(
            (rad.at[p], shift.at[0, :, x_hi], row_send.at[p], row_sem.at[x_hi], target)
        )
    for args in starts:
        send(*args)

    kr, ki = kx[0], kx[1]
    for number_part, part in enumerate(split(jnp.concatenate([kr, ki], axis=1))):
        k2[number_part] = part
    for half_in in range(2):
        for half_out in range(2):
            block_re = ky[0, half_in * 128 : half_in * 128 + 128, half_out * 128 : half_out * 128 + 128]
            block_im = ky[1, half_in * 128 : half_in * 128 + 128, half_out * 128 : half_out * 128 + 128]
            rows = jnp.concatenate(
                [
                    jnp.concatenate([block_re, block_im], axis=1),
                    jnp.concatenate([-block_im, block_re], axis=1),
                ],
                axis=0,
            )
            for number_part, part in enumerate(split(rows)):
                big_y[
                    number_part,
                    half_in * 256 : half_in * 256 + 256,
                    half_out * 256 : half_out * 256 + 256,
                ] = part

    for slot in range(BLOCKS):
        received(el.at[slot], el_sem.at[slot])
    for part in range(2):
        received(shift.at[0, :, part], row_sem.at[part])

    grid_x = lax.broadcasted_iota(jnp.int32, (256, LANES), 0).astype(f32)
    grid_y = (lax.broadcasted_iota(jnp.int32, (128, LANES), 0) + core * 128).astype(f32)

    @pl.loop(0, BLOCKS)
    def _(block):
        for row in range(ROWS):
            index_x = el[block, 2, row : row + 1, :]
            index_y = el[block, 3, row : row + 1, :]
            offset_x = el[block, 4, row : row + 1, :]
            offset_y = el[block, 5, row : row + 1, :]
            lanes = slice(row * LANES, row * LANES + LANES)
            weight = jnp.where(grid_x == index_x, 1.0 - offset_x, 0.0) + jnp.where(
                grid_x == index_x + 1.0, offset_x, 0.0
            )
            hi, lo = split(weight)
            wx[block, 0:256, lanes] = hi
            wx[block, 256:512, lanes] = lo
            wy[block, :, lanes] = jnp.where(grid_y == index_y, 1.0 - offset_y, 0.0) + jnp.where(
                grid_y == index_y + 1.0, offset_y, 0.0
            )
        trig[block, 0] = jnp.cos(el[block, 0])
        trig[block, 1] = jnp.sin(el[block, 0])

    def peer(step):
        other = (q + step) % 8
        return other // 2, other % 2

    def source(step):
        other = (q + 8 - step) % 8
        return other // 2, other % 2

    def gather_copy(n, step):
        to_y, to_core = peer(step)
        return remote(
            shift.at[n, to_core],
            field.at[y, :, core],
            ag_send.at[step],
            ag_sem.at[step],
            role_device(number, to_y, to_core),
        )

    def sums_copy(step):
        to_y, to_core = peer(step)
        return remote(
            mixed.at[to_y, :, to_core],
            sums.at[q],
            rs_send.at[step],
            rs_sem.at[step],
            role_device(number, to_y, to_core),
        )

    def a_copy(block):
        return remote(
            a_send.at[block],
            a_recv.at[block],
            a_ssem.at[block],
            a_rsem.at[block],
            role_device(number, y, 1 - core),
        )

    def out_electrons(part):
        return (
            el_send.at[part],
            el_out.at[number % 2],
            out_send.at[2 + part],
            out_sem.at[2 + number % 2],
            home_device(number, part, y, core),
        )

    def advance(n, last):
        for step in range(1, 8):
            gather_copy(n, step).start()
        field[y, :, core] = shift[n, core]
        for step in range(1, 8):
            from_y, from_core = source(step)
            received(field.at[from_y, :, from_core], ag_sem.at[step])
        full = field[...].reshape(256, 256)
        hi, lo = split(full.T)
        both = jnp.concatenate([hi, lo], axis=0)

        @pl.loop(0, BLOCKS)
        def _(block):
            for row in range(ROWS):
                lanes = slice(row * LANES, row * LANES + LANES)
                first = mm(both, wx[block, 0:256, lanes])
                second = mm(both[0:256], wx[block, 256:512, lanes])
                values = first[0:256] + first[256:512] + second
                weight = wy[block, :, lanes]
                a_send[block, 0, row : row + 1, :] = jnp.sum(
                    values[0:128] * weight, axis=0, keepdims=True
                )
                a_send[block, 1, row : row + 1, :] = jnp.sum(
                    values[128:256] * weight, axis=0, keepdims=True
                )
            a_copy(block).start()

        current[...] = 0.25 * full

        @pl.loop(0, BLOCKS)
        def _(block):
            received(a_recv.at[block], a_rsem.at[block])
            a_re = a_send[block, 0] + a_recv[block, 0]
            a_im = a_send[block, 1] + a_recv[block, 1]
            energy = el[block, 1] - coupling * (a_re * trig[block, 0] - a_im * trig[block, 1])
            phase = el[block, 0] + phase_step * energy
            el[block, 0] = phase
            el[block, 1] = energy
            cos, sin = jnp.cos(phase), jnp.sin(phase)
            trig[block, 0] = cos
            trig[block, 1] = sin
            for row in range(ROWS):
                lanes = slice(row * LANES, row * LANES + LANES)
                weight = current_gain * wy[block, :, lanes]
                values = jnp.concatenate(
                    [weight * cos[row : row + 1, :], -weight * sin[row : row + 1, :]], axis=0
                )
                hi, lo = split(values)
                v_hi[:, lanes] = hi
                v_lo[:, lanes] = lo
            first = mm_nt(wx[block], v_hi[...])
            second = mm_nt(wx[block, 0:256], v_lo[...])
            current[...] += first[0:256] + first[256:512] + second

        if last:
            for part in range(2):
                el_send[part] = el[part * 2 + core, 0:2]
                send(*out_electrons(part))

        total = current[...]
        re, im = total[:, 0:128], total[:, 128:256]
        stacked = jnp.concatenate(
            [total, jnp.concatenate([-im, re], axis=1)], axis=0
        )
        hi, lo = split(stacked)
        product = mm(k2[0], hi) + mm(k2[1], hi) + mm(k2[0], lo)
        mixed[...] = product.reshape(mixed.shape)
        for step in range(1, 8):
            sums_copy(step).start()
        sums[q] = mixed[y, :, core]
        for step in range(1, 8):
            from_y, from_core = source(step)
            received(sums.at[from_y * 2 + from_core], rs_sem.at[step])
        halves = [
            ((sums[half] + sums[half + 2]) + (sums[half + 4] + sums[half + 6])).reshape(32, 256)
            for half in range(2)
        ]
        hi, lo = split(jnp.concatenate(halves, axis=1))
        result = mm(hi, big_y[0]) + mm(hi, big_y[1]) + mm(lo, big_y[0])
        result = jnp.where(following == 0, 0.0, result)
        if last:
            p_out[...] = jnp.concatenate(
                [result[:, 0:128], result[:, 256:384], result[:, 128:256], result[:, 384:512]],
                axis=1,
            ).reshape(p_out.shape)
        else:
            for half in range(2):
                p_send[half] = result[:, half * 256 : half * 256 + 256].reshape(2, 16, 256)
            copy = remote(
                p_send,
                shift.at[n + 1],
                sh_send.at[n],
                sh_sem.at[n],
                role_device(following, y, core),
            )
            copy.start()
        for step in range(1, 8):
            gather_copy(n, step).wait_send()
            sums_copy(step).wait_send()

        @pl.loop(0, BLOCKS)
        def _(block):
            a_copy(block).wait_send()

        if not last:
            copy.wait_send()
            received(shift.at[n + 1], sh_sem.at[n])

    @pl.loop(0, ITERS - 1)
    def _(n):
        advance(n, False)

    advance(ITERS - 1, True)

    def out_rows(part):
        return (
            p_out.at[part],
            rad_out.at[following % 2],
            out_send.at[part],
            out_sem.at[following % 2],
            home_device(following, part, y, core),
        )

    for part in range(2):
        send(*out_rows(part))
    for args in starts:
        sent(*args)
    for part in range(2):
        sent(*out_rows(part))
        sent(*out_electrons(part))
    for part in range(2):
        received(rad_out.at[part], out_sem.at[part])
        received(el_out.at[part], out_sem.at[2 + part])


def shards(radiation, electrons, cell_index, cell_offset, kernel_x, kernel_y):
    rad = radiation.reshape(16, 2, 2, 2, 128).transpose(1, 3, 0, 2, 4).reshape(2, 2, 16, 256)
    el_in = jnp.concatenate([electrons, cell_index.astype(f32), cell_offset], axis=0)
    el_in = el_in.transpose(1, 0, 2).reshape(2, 6, ROWS, LANES)
    vmem = pl.BlockSpec(memory_space=pltpu.VMEM)
    dma = pltpu.SemaphoreType.DMA
    rad_out, el_out = pl.pallas_call(
        kernel,
        out_shape=(
            jax.ShapeDtypeStruct((2, 16, 512), f32),
            jax.ShapeDtypeStruct((2, 2, ROWS, LANES), f32),
        ),
        in_specs=[vmem] * 4,
        out_specs=(vmem, vmem),
        scratch_shapes=[
            pltpu.VMEM((BLOCKS, 6, ROWS, LANES), f32),
            pltpu.VMEM((BLOCKS, 512, ROWS * LANES), bf16),
            pltpu.VMEM((BLOCKS, 128, ROWS * LANES), f32),
            pltpu.VMEM((4, 2, 2, 16, 256), f32),
            pltpu.VMEM((ITERS, 2, 2, 16, 256), f32),
            pltpu.VMEM((BLOCKS, 2, ROWS, LANES), f32),
            pltpu.VMEM((BLOCKS, 2, ROWS, LANES), f32),
            pltpu.VMEM((BLOCKS, 2, ROWS, LANES), f32),
            pltpu.VMEM((256, ROWS * LANES), bf16),
            pltpu.VMEM((256, ROWS * LANES), bf16),
            pltpu.VMEM((256, 256), f32),
            pltpu.VMEM((2, 256, 512), bf16),
            pltpu.VMEM((2, 512, 512), bf16),
            pltpu.VMEM((4, 2, 2, 16, 256), f32),
            pltpu.VMEM((8, 2, 16, 256), f32),
            pltpu.VMEM((2, 2, 16, 256), f32),
            pltpu.VMEM((2, 16, 512), f32),
            pltpu.VMEM((2, 2, ROWS, LANES), f32),
            dma((2, 2)),
            dma((BLOCKS,)),
            dma((2,)),
            dma((2,)),
            dma((8,)),
            dma((8,)),
            dma((BLOCKS,)),
            dma((BLOCKS,)),
            dma((8,)),
            dma((8,)),
            dma((ITERS,)),
            dma((ITERS,)),
            dma((4,)),
            dma((4,)),
        ],
        compiler_params=pltpu.CompilerParams(
            has_side_effects=True, vmem_limit_bytes=48 * 1024 * 1024
        ),
    )(rad, el_in, kernel_x, kernel_y)
    radiation_out = rad_out.transpose(1, 0, 2)
    electrons_out = el_out.reshape(2, 2, ROWS * LANES).transpose(1, 0, 2)
    return radiation_out, electrons_out


def solution(mesh):
    placed = (
        P("dom", "cuts", None),
        P(None, "cuts", "dom"),
        P(None, "cuts", "dom"),
        P(None, "cuts", "dom"),
        P(),
        P(),
    )
    return jax.shard_map(
        shards,
        mesh=mesh,
        in_specs=placed,
        out_specs=(P("dom", "cuts", None), P(None, "cuts", "dom")),
        check_vma=False,
    )
```

```python
import jax
import jax.numpy as jnp
from jax import lax
from jax.experimental import pallas as pl
from jax.experimental.pallas import tpu as pltpu
from jax.sharding import PartitionSpec as P

ITERS = 4
SLICES = 16
coupling = 0.5
phase_step = 1.0
current_gain = 1.0
MESH = pl.DeviceIdType.MESH
f32 = jnp.float32
bf16 = jnp.bfloat16

BLOCKS = 4
ROWS = 8
LANES = 256
ROW_BLOCKS = [
    ((w * 2 + (t + y_lo) % 2) * 2 + core, t)
    for t in range(2)
    for y_lo in range(2)
    for w in range(2)
    for core in range(2)
]


def split(value):
    hi = value.astype(bf16)
    return hi, (value - hi.astype(f32)).astype(bf16)


def mm(a, b):
    return jnp.dot(a, b, preferred_element_type=f32)


def mm_nt(a, b):
    return lax.dot_general(a, b, (((1,), (1,)), ((), ())), preferred_element_type=f32)


def role_device(number, w, u, core):
    pair = number // 2
    x_hi, z = pair // 4, pair % 4
    y_hi = (number % 2 + z) % 2
    x_lo, y_lo = (w + x_hi) % 2, (u + y_hi) % 2
    return x_lo * 4 + z, (y_hi * 2 + y_lo) * 4 + x_hi * 2 + core


def home_device(number, w, t, u, core):
    return number // 2, (t * 2 + (u + t) % 2) * 4 + w * 2 + core


def kernel(
    radiation,
    electrons,
    cell_index,
    cell_offset,
    kx,
    ky,
    radiation_out,
    electrons_out,
    rad,
    el_in,
    rad_back,
    el_back,
    el,
    wx,
    wy,
    field,
    shift,
    a_send,
    a_recv,
    trig,
    v_hi,
    v_lo,
    current,
    k2,
    big_y,
    mixed,
    sums,
    p_send,
    p_out,
    el_send,
    init_send,
    el_sem,
    row_send,
    row_sem,
    ag_send,
    ag_sem,
    a_ssem,
    a_rsem,
    rs_send,
    rs_sem,
    sh_send,
    sh_sem,
    out_send,
    out_sem,
):
    cuts, dom = lax.axis_index("cuts"), lax.axis_index("dom")
    x_lo, z = cuts // 4, cuts % 4
    y, x_hi, core = dom // 4, dom // 2 % 2, dom % 2
    y_hi = y // 2
    w, u = (x_lo + x_hi) % 2, (y + y_hi) % 2
    number = 2 * (x_hi * 4 + z) + (y_hi + z) % 2
    q = (w * 2 + u) * 2 + core
    following = (number + 1) % SLICES
    previous = (number + SLICES - 1) % SLICES

    def peer_device(other):
        return role_device(number, other // 4, other // 2 % 2, other % 2)

    def remote(src, dst, ssem, rsem, device):
        return pltpu.make_async_remote_copy(
            src_ref=src,
            dst_ref=dst,
            send_sem=ssem,
            recv_sem=rsem,
            device_id=device,
            device_id_type=MESH,
        )

    def send(src, dst, ssem, rsem, device):
        self_target = jnp.logical_and(device[0] == cuts, device[1] == dom)

        @pl.when(self_target)
        def _():
            pltpu.make_async_copy(src, dst, rsem).start()

        @pl.when(jnp.logical_not(self_target))
        def _():
            remote(src, dst, ssem, rsem, device).start()

    def sent(src, dst, ssem, rsem, device):
        self_target = jnp.logical_and(device[0] == cuts, device[1] == dom)

        @pl.when(jnp.logical_not(self_target))
        def _():
            remote(src, dst, ssem, rsem, device).wait_send()

    def received(dst, rsem):
        pltpu.make_async_copy(dst, dst, rsem).wait()

    greeted = [peer_device((q + step) % 8) for step in range(1, 8)]
    for a in range(2):
        greeted.append(role_device(2 * cuts + a, x_hi, u, core))
        greeted.append(role_device(2 * cuts + a, x_hi, u, 1 - core))
        greeted.append(home_device(number, w, a, u, core))
        greeted.append(home_device(number, w, a, u, 1 - core))
        greeted.append(home_device(following, w, a, u, core))
        greeted.append(role_device((2 * cuts + a + SLICES - 1) % SLICES, x_hi, u, core))
    greeted.append(role_device(following, w, u, core))
    greeted.append(role_device(previous, w, u, core))
    barrier = pltpu.get_barrier_semaphore()
    expected = 0
    for device in greeted:
        others = jnp.logical_or(device[0] != cuts, device[1] != dom)
        expected = expected + others.astype(jnp.int32)

        @pl.when(others)
        def _():
            pl.semaphore_signal(barrier, inc=1, device_id=device, device_id_type=MESH)

    for p in range(2):
        for half in range(2):
            for part in range(2):
                column = part * 256 + half * 128
                rad[p, half, :, part * 128 : part * 128 + 128] = radiation[
                    :, p, column : column + 128
                ]
        for row in range(ROWS):
            lanes = slice(row * LANES, row * LANES + LANES)
            for field_number in range(2):
                place = slice(row, row + 1)
                el_in[p, field_number, place] = electrons[field_number, p : p + 1, lanes]
                el_in[p, 2 + field_number, place] = cell_index[
                    field_number, p : p + 1, lanes
                ].astype(f32)
                el_in[p, 4 + field_number, place] = cell_offset[field_number, p : p + 1, lanes]
    pl.semaphore_wait(barrier, expected)

    own_slot = y_hi * 2 + core
    starts = []
    for p in range(2):
        starts.append(
            (
                rad.at[p],
                shift.at[0, :, y_hi],
                row_send.at[p],
                row_sem.at[y_hi],
                role_device(2 * cuts + p, x_hi, u, core),
            )
        )
    for p in range(2):
        for number_core in range(2):
            starts.append(
                (
                    el_in.at[p],
                    el.at[own_slot],
                    init_send.at[p, number_core],
                    el_sem.at[own_slot],
                    role_device(2 * cuts + p, x_hi, u, (core + number_core) % 2),
                )
            )
    for args in starts:
        send(*args)

    kr, ki = kx[0], kx[1]
    for number_part, part in enumerate(split(jnp.concatenate([kr, ki], axis=1))):
        k2[number_part] = part
    for half_in in range(2):
        for half_out in range(2):
            block_re = ky[0, half_in * 128 : half_in * 128 + 128, half_out * 128 : half_out * 128 + 128]
            block_im = ky[1, half_in * 128 : half_in * 128 + 128, half_out * 128 : half_out * 128 + 128]
            rows = jnp.concatenate(
                [
                    jnp.concatenate([block_re, block_im], axis=1),
                    jnp.concatenate([-block_im, block_re], axis=1),
                ],
                axis=0,
            )
            for number_part, part in enumerate(split(rows)):
                big_y[
                    number_part,
                    half_in * 256 : half_in * 256 + 256,
                    half_out * 256 : half_out * 256 + 256,
                ] = part

    def peer(step):
        return (q + step) % 8

    def source(step):
        return (q + 8 - step) % 8

    def gather_copy(n, step):
        to = peer(step)
        return remote(
            shift.at[n, to % 2],
            field.at[q],
            ag_send.at[step],
            ag_sem.at[step],
            peer_device(to),
        )

    def sums_copy(step):
        to = peer(step)
        return remote(
            mixed.at[to], sums.at[q], rs_send.at[step], rs_sem.at[step], peer_device(to)
        )

    def start_gather(n):
        for step in range(1, 8):
            gather_copy(n, step).start()
        field[q] = shift[n, core]

    def a_copy(block):
        return remote(
            a_send.at[block],
            a_recv.at[block],
            a_ssem.at[block],
            a_rsem.at[block],
            role_device(number, w, u, 1 - core),
        )

    def out_electrons(part):
        return (
            el_send.at[part],
            el_back.at[number % 2],
            out_send.at[2 + part],
            out_sem.at[2 + number % 2],
            home_device(number, w, part, u, core),
        )

    def advance(n, last):
        for step in range(1, 8):
            received(field.at[source(step)], ag_sem.at[step])
        full = jnp.concatenate([field[owner, part] for owner, part in ROW_BLOCKS], axis=0)
        hi, lo = split(full.T)
        both = jnp.concatenate([hi, lo], axis=0)

        @pl.loop(0, BLOCKS)
        def _(block):
            for row in range(ROWS):
                lanes = slice(row * LANES, row * LANES + LANES)
                first = mm(both, wx[block, 0:256, lanes])
                second = mm(both[0:256], wx[block, 256:512, lanes])
                values = first[0:256] + first[256:512] + second
                weight = wy[block, :, lanes]
                a_send[block, 0, row : row + 1, :] = jnp.sum(
                    values[0:128] * weight, axis=0, keepdims=True
                )
                a_send[block, 1, row : row + 1, :] = jnp.sum(
                    values[128:256] * weight, axis=0, keepdims=True
                )
            a_copy(block).start()

        current[...] = 0.25 * full

        @pl.loop(0, BLOCKS)
        def _(block):
            received(a_recv.at[block], a_rsem.at[block])
            a_re = a_send[block, 0] + a_recv[block, 0]
            a_im = a_send[block, 1] + a_recv[block, 1]
            energy = el[block, 1] - coupling * (a_re * trig[block, 0] - a_im * trig[block, 1])
            phase = el[block, 0] + phase_step * energy
            el[block, 0] = phase
            el[block, 1] = energy
            cos, sin = jnp.cos(phase), jnp.sin(phase)
            trig[block, 0] = cos
            trig[block, 1] = sin
            for row in range(ROWS):
                lanes = slice(row * LANES, row * LANES + LANES)
                weight = current_gain * wy[block, :, lanes]
                values = jnp.concatenate(
                    [weight * cos[row : row + 1, :], -weight * sin[row : row + 1, :]], axis=0
                )
                hi, lo = split(values)
                v_hi[:, lanes] = hi
                v_lo[:, lanes] = lo
            first = mm_nt(wx[block], v_hi[...])
            second = mm_nt(wx[block, 0:256], v_lo[...])
            current[...] += first[0:256] + first[256:512] + second

        if last:
            for part in range(2):
                el_send[part] = el[part * 2 + core, 0:2]
                send(*out_electrons(part))

        total = current[...]
        re, im = total[:, 0:128], total[:, 128:256]
        stacked = jnp.concatenate(
            [total, jnp.concatenate([-im, re], axis=1)], axis=0
        )
        hi, lo = split(stacked)
        product = mm(k2[0], hi) + mm(k2[1], hi) + mm(k2[0], lo)
        for place, (owner, part) in enumerate(ROW_BLOCKS):
            mixed[owner, part] = product[place * 16 : place * 16 + 16]
        for step in range(1, 8):
            sums_copy(step).start()
        sums[q] = mixed[q]
        for step in range(1, 8):
            received(sums.at[source(step)], rs_sem.at[step])
        halves = [
            ((sums[half] + sums[half + 2]) + (sums[half + 4] + sums[half + 6])).reshape(32, 256)
            for half in range(2)
        ]
        hi, lo = split(jnp.concatenate(halves, axis=1))
        result = mm(hi, big_y[0]) + mm(hi, big_y[1]) + mm(lo, big_y[0])
        result = jnp.where(following == 0, 0.0, result)
        if last:
            p_out[...] = jnp.concatenate(
                [result[:, 0:128], result[:, 256:384], result[:, 128:256], result[:, 384:512]],
                axis=1,
            ).reshape(p_out.shape)
        else:
            for half in range(2):
                p_send[half] = result[:, half * 256 : half * 256 + 256].reshape(2, 16, 256)
            copy = remote(
                p_send,
                shift.at[n + 1],
                sh_send.at[n],
                sh_sem.at[n],
                role_device(following, w, u, core),
            )
            copy.start()
        for step in range(1, 8):
            gather_copy(n, step).wait_send()
            sums_copy(step).wait_send()

        @pl.loop(0, BLOCKS)
        def _(block):
            a_copy(block).wait_send()

        if not last:
            copy.wait_send()
            received(shift.at[n + 1], sh_sem.at[n])
            start_gather(n + 1)

    for part in range(2):
        received(shift.at[0, :, part], row_sem.at[part])
    start_gather(0)
    for slot in range(BLOCKS):
        received(el.at[slot], el_sem.at[slot])

    grid_x = lax.broadcasted_iota(jnp.int32, (256, LANES), 0).astype(f32)
    grid_y = (lax.broadcasted_iota(jnp.int32, (128, LANES), 0) + core * 128).astype(f32)

    @pl.loop(0, BLOCKS)
    def _(block):
        for row in range(ROWS):
            index_x = el[block, 2, row : row + 1, :]
            index_y = el[block, 3, row : row + 1, :]
            offset_x = el[block, 4, row : row + 1, :]
            offset_y = el[block, 5, row : row + 1, :]
            lanes = slice(row * LANES, row * LANES + LANES)
            weight = jnp.where(grid_x == index_x, 1.0 - offset_x, 0.0) + jnp.where(
                grid_x == index_x + 1.0, offset_x, 0.0
            )
            hi, lo = split(weight)
            wx[block, 0:256, lanes] = hi
            wx[block, 256:512, lanes] = lo
            wy[block, :, lanes] = jnp.where(grid_y == index_y, 1.0 - offset_y, 0.0) + jnp.where(
                grid_y == index_y + 1.0, offset_y, 0.0
            )
        trig[block, 0] = jnp.cos(el[block, 0])
        trig[block, 1] = jnp.sin(el[block, 0])

    @pl.loop(0, ITERS - 1)
    def _(n):
        advance(n, False)

    advance(ITERS - 1, True)

    def out_rows(part):
        return (
            p_out.at[part],
            rad_back.at[following % 2],
            out_send.at[part],
            out_sem.at[following % 2],
            home_device(following, w, part, u, core),
        )

    for part in range(2):
        send(*out_rows(part))
    for args in starts:
        sent(*args)
    for part in range(2):
        sent(*out_rows(part))
        sent(*out_electrons(part))
    for part in range(2):
        received(rad_back.at[part], out_sem.at[part])
        received(el_back.at[part], out_sem.at[2 + part])
    for p in range(2):
        radiation_out[:, p, :] = rad_back[p]
        for row in range(ROWS):
            lanes = slice(row * LANES, row * LANES + LANES)
            for field_number in range(2):
                electrons_out[field_number, p : p + 1, lanes] = el_back[
                    p, field_number, row : row + 1
                ]


def shards(radiation, electrons, cell_index, cell_offset, kernel_x, kernel_y):
    vmem = pl.BlockSpec(memory_space=pltpu.VMEM)
    dma = pltpu.SemaphoreType.DMA
    return pl.pallas_call(
        kernel,
        out_shape=(
            jax.ShapeDtypeStruct(radiation.shape, f32),
            jax.ShapeDtypeStruct(electrons.shape, f32),
        ),
        in_specs=[vmem] * 6,
        out_specs=(vmem, vmem),
        scratch_shapes=[
            pltpu.VMEM((2, 2, 16, 256), f32),
            pltpu.VMEM((2, 6, ROWS, LANES), f32),
            pltpu.VMEM((2, 16, 512), f32),
            pltpu.VMEM((2, 2, ROWS, LANES), f32),
            pltpu.VMEM((BLOCKS, 6, ROWS, LANES), f32),
            pltpu.VMEM((BLOCKS, 512, ROWS * LANES), bf16),
            pltpu.VMEM((BLOCKS, 128, ROWS * LANES), f32),
            pltpu.VMEM((8, 2, 16, 256), f32),
            pltpu.VMEM((ITERS, 2, 2, 16, 256), f32),
            pltpu.VMEM((BLOCKS, 2, ROWS, LANES), f32),
            pltpu.VMEM((BLOCKS, 2, ROWS, LANES), f32),
            pltpu.VMEM((BLOCKS, 2, ROWS, LANES), f32),
            pltpu.VMEM((256, ROWS * LANES), bf16),
            pltpu.VMEM((256, ROWS * LANES), bf16),
            pltpu.VMEM((256, 256), f32),
            pltpu.VMEM((2, 256, 512), bf16),
            pltpu.VMEM((2, 512, 512), bf16),
            pltpu.VMEM((8, 2, 16, 256), f32),
            pltpu.VMEM((8, 2, 16, 256), f32),
            pltpu.VMEM((2, 2, 16, 256), f32),
            pltpu.VMEM((2, 16, 512), f32),
            pltpu.VMEM((2, 2, ROWS, LANES), f32),
            dma((2, 2)),
            dma((BLOCKS,)),
            dma((2,)),
            dma((2,)),
            dma((8,)),
            dma((8,)),
            dma((BLOCKS,)),
            dma((BLOCKS,)),
            dma((8,)),
            dma((8,)),
            dma((ITERS,)),
            dma((ITERS,)),
            dma((4,)),
            dma((4,)),
        ],
        compiler_params=pltpu.CompilerParams(
            collective_id=0, has_side_effects=True, vmem_limit_bytes=48 * 1024 * 1024
        ),
    )(radiation, electrons, cell_index, cell_offset, kernel_x, kernel_y)


def solution(mesh):
    placed = (
        P("dom", "cuts", None),
        P(None, "cuts", "dom"),
        P(None, "cuts", "dom"),
        P(None, "cuts", "dom"),
        P(),
        P(),
    )
    return jax.shard_map(
        shards,
        mesh=mesh,
        in_specs=placed,
        out_specs=(P("dom", "cuts", None), P(None, "cuts", "dom")),
        check_vma=False,
    )
```

```python
import jax
import jax.numpy as jnp
from jax import lax
from jax.experimental import pallas as pl
from jax.experimental.pallas import tpu as pltpu
from jax.sharding import PartitionSpec as P

ITERS = 4
SLICES = 16
coupling = 0.5
phase_step = 1.0
current_gain = 1.0
MESH = pl.DeviceIdType.MESH
f32 = jnp.float32
bf16 = jnp.bfloat16

BLOCKS = 4
ROWS = 8
LANES = 256
ROW_BLOCKS = [
    ((w * 2 + (t + y_lo) % 2) * 2 + core, t)
    for t in range(2)
    for y_lo in range(2)
    for w in range(2)
    for core in range(2)
]


def split(value):
    hi = value.astype(bf16)
    return hi, (value - hi.astype(f32)).astype(bf16)


def mm(a, b):
    return jnp.dot(a, b, preferred_element_type=f32)


def mm_nt(a, b):
    return lax.dot_general(a, b, (((1,), (1,)), ((), ())), preferred_element_type=f32)


def role_device(number, w, u, core):
    pair = number // 2
    x_hi, z = pair // 4, pair % 4
    y_hi = (number % 2 + z) % 2
    x_lo, y_lo = (w + x_hi) % 2, (u + y_hi) % 2
    return x_lo * 4 + z, (y_hi * 2 + y_lo) * 4 + x_hi * 2 + core


def home_device(number, w, t, u, core):
    return number // 2, (t * 2 + (u + t) % 2) * 4 + w * 2 + core


def kernel(
    radiation,
    electrons,
    cell_index,
    cell_offset,
    kx,
    ky,
    radiation_out,
    electrons_out,
    rad,
    el_in,
    rad_back,
    el_back,
    el,
    wx,
    wy,
    field,
    a_send,
    a_recv,
    trig,
    v_hi,
    v_lo,
    current,
    k2,
    big_y,
    mixed,
    sums,
    p_send,
    p_out,
    el_send,
    init_send,
    el_sem,
    row_send,
    row_sem,
    ag_send,
    ag_sem,
    a_ssem,
    a_rsem,
    rs_send,
    rs_sem,
    place_send,
    place_sem,
    state_send,
    state_sem,
    out_send,
    out_sem,
):
    cuts, dom = lax.axis_index("cuts"), lax.axis_index("dom")
    x_lo, z = cuts // 4, cuts % 4
    y, x_hi, core = dom // 4, dom // 2 % 2, dom % 2
    y_hi = y // 2
    w, u = (x_lo + x_hi) % 2, (y + y_hi) % 2
    number = 2 * (x_hi * 4 + z) + (y_hi + z) % 2
    q = (w * 2 + u) * 2 + core
    last_number = (number + ITERS - 1) % SLICES
    row_number = (number + ITERS) % SLICES

    def peer_device(other):
        return role_device(number, other // 4, other // 2 % 2, other % 2)

    peers = [peer_device((q + step) % 8) for step in range(8)]
    beside = peer_device(q + 1 - 2 * core)
    ahead = role_device((number + SLICES - 1) % SLICES, w, u, core)

    def remote(src, dst, ssem, rsem, device):
        return pltpu.make_async_remote_copy(
            src_ref=src,
            dst_ref=dst,
            send_sem=ssem,
            recv_sem=rsem,
            device_id=device,
            device_id_type=MESH,
        )

    def send(src, dst, ssem, rsem, device):
        self_target = jnp.logical_and(device[0] == cuts, device[1] == dom)

        @pl.when(self_target)
        def _():
            pltpu.make_async_copy(src, dst, rsem).start()

        @pl.when(jnp.logical_not(self_target))
        def _():
            remote(src, dst, ssem, rsem, device).start()

    def sent(src, dst, ssem, rsem, device):
        self_target = jnp.logical_and(device[0] == cuts, device[1] == dom)

        @pl.when(jnp.logical_not(self_target))
        def _():
            remote(src, dst, ssem, rsem, device).wait_send()

    def received(dst, rsem):
        pltpu.make_async_copy(dst, dst, rsem).wait()

    greeted = peers[1:]
    for a in range(2):
        greeted.append(role_device(2 * cuts + a, x_hi, u, core))
        greeted.append(role_device(2 * cuts + a, x_hi, u, 1 - core))
        greeted.append(home_device(number, w, a, u, core))
        greeted.append(home_device(number, w, a, u, 1 - core))
        for moved, end in ((ITERS - 1, last_number), (ITERS, row_number)):
            greeted.append(home_device(end, w, a, u, core))
            greeted.append(role_device((2 * cuts + a + SLICES - moved) % SLICES, x_hi, u, core))
    greeted.append(ahead)
    greeted.append(role_device((number + 1) % SLICES, w, u, core))
    barrier = pltpu.get_barrier_semaphore()
    expected = 0
    for device in greeted:
        others = jnp.logical_or(device[0] != cuts, device[1] != dom)
        expected = expected + others.astype(jnp.int32)

        @pl.when(others)
        def _():
            pl.semaphore_signal(barrier, inc=1, device_id=device, device_id_type=MESH)

    for p in range(2):
        for half in range(2):
            for part in range(2):
                column = part * 256 + half * 128
                rad[p, half, :, part * 128 : part * 128 + 128] = radiation[
                    :, p, column : column + 128
                ]
        for row in range(ROWS):
            lanes = slice(row * LANES, row * LANES + LANES)
            for field_number in range(2):
                place = slice(row, row + 1)
                el_in[p, field_number, place] = electrons[field_number, p : p + 1, lanes]
                el_in[p, 2 + field_number, place] = cell_index[
                    field_number, p : p + 1, lanes
                ].astype(f32)
                el_in[p, 4 + field_number, place] = cell_offset[field_number, p : p + 1, lanes]
    pl.semaphore_wait(barrier, expected)

    own_slot = y_hi * 2 + core
    starts = []
    for p in range(2):
        starts.append(
            (
                rad.at[p],
                p_send.at[:, y_hi],
                row_send.at[p],
                row_sem.at[y_hi],
                role_device(2 * cuts + p, x_hi, u, core),
            )
        )
    for p in range(2):
        for number_core in range(2):
            starts.append(
                (
                    el_in.at[p],
                    el.at[0, own_slot],
                    init_send.at[p, number_core],
                    el_sem.at[own_slot],
                    role_device(2 * cuts + p, x_hi, u, (core + number_core) % 2),
                )
            )
    for args in starts:
        send(*args)

    kr, ki = kx[0], kx[1]
    for number_part, part in enumerate(split(jnp.concatenate([kr, ki], axis=1))):
        k2[number_part] = part
    for half_in in range(2):
        for half_out in range(2):
            block_re = ky[0, half_in * 128 : half_in * 128 + 128, half_out * 128 : half_out * 128 + 128]
            block_im = ky[1, half_in * 128 : half_in * 128 + 128, half_out * 128 : half_out * 128 + 128]
            rows = jnp.concatenate(
                [
                    jnp.concatenate([block_re, block_im], axis=1),
                    jnp.concatenate([-block_im, block_re], axis=1),
                ],
                axis=0,
            )
            for number_part, part in enumerate(split(rows)):
                big_y[
                    number_part,
                    half_in * 256 : half_in * 256 + 256,
                    half_out * 256 : half_out * 256 + 256,
                ] = part

    def gather_copy(step):
        return remote(
            p_send.at[(core + step) % 2],
            field.at[q],
            ag_send.at[step],
            ag_sem.at[step],
            peers[step],
        )

    def sums_copy(step):
        return remote(
            mixed.at[(q + step) % 8], sums.at[q], rs_send.at[step], rs_sem.at[step], peers[step]
        )

    def start_gather():
        for step in range(1, 8):
            gather_copy(step).start()
        field[q] = p_send[core]

    def a_copy(block):
        return remote(
            a_send.at[block], a_recv.at[block], a_ssem.at[block], a_rsem.at[block], beside
        )

    def place_copy(n):
        return remote(
            el.at[n, :, 2:6], el.at[n + 1, :, 2:6], place_send.at[n], place_sem.at[n], ahead
        )

    def state_copy(n, block):
        return remote(
            el.at[n, block, 0:2],
            el.at[n + 1, block, 0:2],
            state_send.at[n, block],
            state_sem.at[n, block],
            ahead,
        )

    def out_electrons(part):
        return (
            el_send.at[part],
            el_back.at[last_number % 2],
            out_send.at[2 + part],
            out_sem.at[2 + last_number % 2],
            home_device(last_number, w, part, u, core),
        )

    def build(n):
        @pl.loop(0, BLOCKS)
        def _(block):
            for row in range(ROWS):
                index_x = el[n, block, 2, row : row + 1, :]
                index_y = el[n, block, 3, row : row + 1, :]
                offset_x = el[n, block, 4, row : row + 1, :]
                offset_y = el[n, block, 5, row : row + 1, :]
                lanes = slice(row * LANES, row * LANES + LANES)
                grid_x = lax.broadcasted_iota(jnp.int32, (256, LANES), 0).astype(f32)
                grid_y = (lax.broadcasted_iota(jnp.int32, (128, LANES), 0) + core * 128).astype(f32)
                weight = jnp.where(grid_x == index_x, 1.0 - offset_x, 0.0) + jnp.where(
                    grid_x == index_x + 1.0, offset_x, 0.0
                )
                hi, lo = split(weight)
                wx[block, 0:256, lanes] = hi
                wx[block, 256:512, lanes] = lo
                wy[block, :, lanes] = jnp.where(
                    grid_y == index_y, 1.0 - offset_y, 0.0
                ) + jnp.where(grid_y == index_y + 1.0, offset_y, 0.0)
            trig[block, 0] = jnp.cos(el[n, block, 0])
            trig[block, 1] = jnp.sin(el[n, block, 0])

    def advance(n, last):
        if not last:
            place_copy(n).start()
        for step in range(1, 8):
            received(field.at[(q + 8 - step) % 8], ag_sem.at[step])
        full = jnp.concatenate([field[owner, part] for owner, part in ROW_BLOCKS], axis=0)
        hi, lo = split(full.T)
        both = jnp.concatenate([hi, lo], axis=0)

        @pl.loop(0, BLOCKS)
        def _(block):
            for row in range(ROWS):
                lanes = slice(row * LANES, row * LANES + LANES)
                first = mm(both, wx[block, 0:256, lanes])
                second = mm(both[0:256], wx[block, 256:512, lanes])
                values = first[0:256] + first[256:512] + second
                weight = wy[block, :, lanes]
                a_send[block, 0, row : row + 1, :] = jnp.sum(
                    values[0:128] * weight, axis=0, keepdims=True
                )
                a_send[block, 1, row : row + 1, :] = jnp.sum(
                    values[128:256] * weight, axis=0, keepdims=True
                )
            a_copy(block).start()

        current[...] = 0.25 * full

        @pl.loop(0, BLOCKS)
        def _(block):
            received(a_recv.at[block], a_rsem.at[block])
            a_re = a_send[block, 0] + a_recv[block, 0]
            a_im = a_send[block, 1] + a_recv[block, 1]
            energy = el[n, block, 1] - coupling * (a_re * trig[block, 0] - a_im * trig[block, 1])
            phase = el[n, block, 0] + phase_step * energy
            el[n, block, 0] = phase
            el[n, block, 1] = energy
            if not last:
                state_copy(n, block).start()
            cos, sin = jnp.cos(phase), jnp.sin(phase)
            for row in range(ROWS):
                lanes = slice(row * LANES, row * LANES + LANES)
                weight = current_gain * wy[block, :, lanes]
                values = jnp.concatenate(
                    [weight * cos[row : row + 1, :], -weight * sin[row : row + 1, :]], axis=0
                )
                hi, lo = split(values)
                v_hi[:, lanes] = hi
                v_lo[:, lanes] = lo
            first = mm_nt(wx[block], v_hi[...])
            second = mm_nt(wx[block, 0:256], v_lo[...])
            current[...] += first[0:256] + first[256:512] + second

        if last:
            for part in range(2):
                el_send[part] = el[n, part * 2 + core, 0:2]
                send(*out_electrons(part))

        total = current[...]
        re, im = total[:, 0:128], total[:, 128:256]
        stacked = jnp.concatenate([total, jnp.concatenate([-im, re], axis=1)], axis=0)
        hi, lo = split(stacked)
        product = mm(k2[0], hi) + mm(k2[1], hi) + mm(k2[0], lo)
        for index, (owner, part) in enumerate(ROW_BLOCKS):
            mixed[owner, part] = product[index * 16 : index * 16 + 16]
        for step in range(1, 8):
            sums_copy(step).start()
        sums[q] = mixed[q]
        if not last:
            received(el.at[n + 1, :, 2:6], place_sem.at[n])

            @pl.loop(0, BLOCKS)
            def _(block):
                received(el.at[n + 1, block, 0:2], state_sem.at[n, block])

            build(n + 1)
        for step in range(1, 8):
            received(sums.at[(q + 8 - step) % 8], rs_sem.at[step])
        halves = [
            ((sums[half] + sums[half + 2]) + (sums[half + 4] + sums[half + 6])).reshape(32, 256)
            for half in range(2)
        ]
        hi, lo = split(jnp.concatenate(halves, axis=1))
        result = mm(hi, big_y[0]) + mm(hi, big_y[1]) + mm(lo, big_y[0])
        result = jnp.where((number + n + 1) % SLICES == 0, 0.0, result)
        for step in range(1, 8):
            gather_copy(step).wait_send()
            sums_copy(step).wait_send()
        if last:
            p_out[...] = jnp.concatenate(
                [result[:, 0:128], result[:, 256:384], result[:, 128:256], result[:, 384:512]],
                axis=1,
            ).reshape(p_out.shape)
        else:
            for half in range(2):
                p_send[half] = result[:, half * 256 : half * 256 + 256].reshape(2, 16, 256)
            start_gather()
            place_copy(n).wait_send()

        @pl.loop(0, BLOCKS)
        def _(block):
            a_copy(block).wait_send()
            if not last:
                state_copy(n, block).wait_send()

    for part in range(2):
        received(p_send.at[:, part], row_sem.at[part])
    start_gather()
    for slot in range(BLOCKS):
        received(el.at[0, slot], el_sem.at[slot])
    build(0)

    @pl.loop(0, ITERS - 1)
    def _(n):
        advance(n, False)

    advance(ITERS - 1, True)

    def out_rows(part):
        return (
            p_out.at[part],
            rad_back.at[row_number % 2],
            out_send.at[part],
            out_sem.at[row_number % 2],
            home_device(row_number, w, part, u, core),
        )

    for part in range(2):
        send(*out_rows(part))
    for args in starts:
        sent(*args)
    for part in range(2):
        sent(*out_rows(part))
        sent(*out_electrons(part))
    for part in range(2):
        received(rad_back.at[part], out_sem.at[part])
        received(el_back.at[part], out_sem.at[2 + part])
    for p in range(2):
        radiation_out[:, p, :] = rad_back[p]
        for row in range(ROWS):
            lanes = slice(row * LANES, row * LANES + LANES)
            for field_number in range(2):
                electrons_out[field_number, p : p + 1, lanes] = el_back[
                    p, field_number, row : row + 1
                ]


def shards(radiation, electrons, cell_index, cell_offset, kernel_x, kernel_y):
    vmem = pl.BlockSpec(memory_space=pltpu.VMEM)
    dma = pltpu.SemaphoreType.DMA
    return pl.pallas_call(
        kernel,
        out_shape=(
            jax.ShapeDtypeStruct(radiation.shape, f32),
            jax.ShapeDtypeStruct(electrons.shape, f32),
        ),
        in_specs=[vmem] * 6,
        out_specs=(vmem, vmem),
        scratch_shapes=[
            pltpu.VMEM((2, 2, 16, 256), f32),
            pltpu.VMEM((2, 6, ROWS, LANES), f32),
            pltpu.VMEM((2, 16, 512), f32),
            pltpu.VMEM((2, 2, ROWS, LANES), f32),
            pltpu.VMEM((ITERS, BLOCKS, 6, ROWS, LANES), f32),
            pltpu.VMEM((BLOCKS, 512, ROWS * LANES), bf16),
            pltpu.VMEM((BLOCKS, 128, ROWS * LANES), f32),
            pltpu.VMEM((8, 2, 16, 256), f32),
            pltpu.VMEM((BLOCKS, 2, ROWS, LANES), f32),
            pltpu.VMEM((BLOCKS, 2, ROWS, LANES), f32),
            pltpu.VMEM((BLOCKS, 2, ROWS, LANES), f32),
            pltpu.VMEM((256, ROWS * LANES), bf16),
            pltpu.VMEM((256, ROWS * LANES), bf16),
            pltpu.VMEM((256, 256), f32),
            pltpu.VMEM((2, 256, 512), bf16),
            pltpu.VMEM((2, 512, 512), bf16),
            pltpu.VMEM((8, 2, 16, 256), f32),
            pltpu.VMEM((8, 2, 16, 256), f32),
            pltpu.VMEM((2, 2, 16, 256), f32),
            pltpu.VMEM((2, 16, 512), f32),
            pltpu.VMEM((2, 2, ROWS, LANES), f32),
            dma((2, 2)),
            dma((BLOCKS,)),
            dma((2,)),
            dma((2,)),
            dma((8,)),
            dma((8,)),
            dma((BLOCKS,)),
            dma((BLOCKS,)),
            dma((8,)),
            dma((8,)),
            dma((ITERS,)),
            dma((ITERS,)),
            dma((ITERS, BLOCKS)),
            dma((ITERS, BLOCKS)),
            dma((4,)),
            dma((4,)),
        ],
        compiler_params=pltpu.CompilerParams(
            collective_id=0, has_side_effects=True, vmem_limit_bytes=48 * 1024 * 1024
        ),
    )(radiation, electrons, cell_index, cell_offset, kernel_x, kernel_y)


def solution(mesh):
    placed = (
        P("dom", "cuts", None),
        P(None, "cuts", "dom"),
        P(None, "cuts", "dom"),
        P(None, "cuts", "dom"),
        P(),
        P(),
    )
    return jax.shard_map(
        shards,
        mesh=mesh,
        in_specs=placed,
        out_specs=(P("dom", "cuts", None), P(None, "cuts", "dom")),
        check_vma=False,
    )
```

```python
import jax
import jax.numpy as jnp
from jax import lax
from jax.experimental import pallas as pl
from jax.experimental.pallas import tpu as pltpu
from jax.sharding import PartitionSpec as P

ITERS = 4
SLICES = 16
coupling = 0.5
phase_step = 1.0
current_gain = 1.0
MESH = pl.DeviceIdType.MESH
f32 = jnp.float32
bf16 = jnp.bfloat16

BLOCKS = 4
ROWS = 8
LANES = 256
ROW_BLOCKS = [
    ((w * 2 + (t + y_lo) % 2) * 2 + core, t)
    for t in range(2)
    for y_lo in range(2)
    for w in range(2)
    for core in range(2)
]


def split(value):
    hi = value.astype(bf16)
    return hi, (value - hi.astype(f32)).astype(bf16)


def mm(a, b):
    return jnp.dot(a, b, preferred_element_type=f32)


def mm_nt(a, b):
    return lax.dot_general(a, b, (((1,), (1,)), ((), ())), preferred_element_type=f32)


def role_device(number, w, u, core):
    pair = number // 2
    x_hi, z = pair // 4, pair % 4
    y_hi = (number % 2 + z) % 2
    x_lo, y_lo = (w + x_hi) % 2, (u + y_hi) % 2
    return x_lo * 4 + z, (y_hi * 2 + y_lo) * 4 + x_hi * 2 + core


def home_device(number, w, t, u, core):
    return number // 2, (t * 2 + (u + t) % 2) * 4 + w * 2 + core


def kernel(
    radiation_hbm,
    electrons_hbm,
    cell_index_hbm,
    cell_offset_hbm,
    kx_hbm,
    ky_hbm,
    radiation_out,
    electrons_out,
    radiation,
    electrons,
    cell_index,
    cell_offset,
    kx,
    ky,
    rad,
    el_in,
    rad_back,
    el_back,
    el,
    wx,
    wy,
    field,
    a_send,
    a_recv,
    trig,
    v_hi,
    v_lo,
    current,
    k2,
    big_y,
    mixed,
    sums,
    p_send,
    p_out,
    el_send,
    init_send,
    el_sem,
    row_send,
    row_sem,
    ag_send,
    ag_sem,
    a_ssem,
    a_rsem,
    rs_send,
    rs_sem,
    place_send,
    place_sem,
    state_send,
    state_sem,
    out_send,
    out_sem,
    in_sem,
):
    cuts, dom = lax.axis_index("cuts"), lax.axis_index("dom")
    x_lo, z = cuts // 4, cuts % 4
    y, x_hi, core = dom // 4, dom // 2 % 2, dom % 2
    y_hi = y // 2
    w, u = (x_lo + x_hi) % 2, (y + y_hi) % 2
    number = 2 * (x_hi * 4 + z) + (y_hi + z) % 2
    q = (w * 2 + u) * 2 + core
    last_number = (number + ITERS - 1) % SLICES
    row_number = (number + ITERS) % SLICES

    def peer_device(other):
        return role_device(number, other // 4, other // 2 % 2, other % 2)

    peers = [peer_device((q + step) % 8) for step in range(8)]
    beside = peer_device(q + 1 - 2 * core)
    ahead = role_device((number + SLICES - 1) % SLICES, w, u, core)

    def remote(src, dst, ssem, rsem, device):
        return pltpu.make_async_remote_copy(
            src_ref=src,
            dst_ref=dst,
            send_sem=ssem,
            recv_sem=rsem,
            device_id=device,
            device_id_type=MESH,
        )

    def send(src, dst, ssem, rsem, device):
        self_target = jnp.logical_and(device[0] == cuts, device[1] == dom)

        @pl.when(self_target)
        def _():
            pltpu.make_async_copy(src, dst, rsem).start()

        @pl.when(jnp.logical_not(self_target))
        def _():
            remote(src, dst, ssem, rsem, device).start()

    def sent(src, dst, ssem, rsem, device):
        self_target = jnp.logical_and(device[0] == cuts, device[1] == dom)

        @pl.when(jnp.logical_not(self_target))
        def _():
            remote(src, dst, ssem, rsem, device).wait_send()

    def received(dst, rsem):
        pltpu.make_async_copy(dst, dst, rsem).wait()

    greeted = peers[1:]
    for a in range(2):
        greeted.append(role_device(2 * cuts + a, x_hi, u, core))
        greeted.append(role_device(2 * cuts + a, x_hi, u, 1 - core))
        greeted.append(home_device(number, w, a, u, core))
        greeted.append(home_device(number, w, a, u, 1 - core))
        for moved, end in ((ITERS - 1, last_number), (ITERS, row_number)):
            greeted.append(home_device(end, w, a, u, core))
            greeted.append(role_device((2 * cuts + a + SLICES - moved) % SLICES, x_hi, u, core))
    greeted.append(ahead)
    greeted.append(role_device((number + 1) % SLICES, w, u, core))
    barrier = pltpu.get_barrier_semaphore()
    expected = 0
    for device in greeted:
        others = jnp.logical_or(device[0] != cuts, device[1] != dom)
        expected = expected + others.astype(jnp.int32)

        @pl.when(others)
        def _():
            pl.semaphore_signal(barrier, inc=1, device_id=device, device_id_type=MESH)

    loads = [
        pltpu.make_async_copy(src, dst, in_sem.at[index])
        for index, (src, dst) in enumerate(
            [
                (radiation_hbm, radiation),
                (electrons_hbm, electrons),
                (cell_index_hbm, cell_index),
                (cell_offset_hbm, cell_offset),
                (kx_hbm, kx),
                (ky_hbm, ky),
            ]
        )
    ]
    for load in loads:
        load.start()
    for load in loads[0:4]:
        load.wait()
    for p in range(2):
        for half in range(2):
            for part in range(2):
                column = part * 256 + half * 128
                rad[p, half, :, part * 128 : part * 128 + 128] = radiation[
                    :, p, column : column + 128
                ]
        for row in range(ROWS):
            lanes = slice(row * LANES, row * LANES + LANES)
            for field_number in range(2):
                place = slice(row, row + 1)
                el_in[p, field_number, place] = electrons[field_number, p : p + 1, lanes]
                el_in[p, 2 + field_number, place] = cell_index[
                    field_number, p : p + 1, lanes
                ].astype(f32)
                el_in[p, 4 + field_number, place] = cell_offset[field_number, p : p + 1, lanes]
    pl.semaphore_wait(barrier, expected)

    own_slot = y_hi * 2 + core
    starts = []
    for p in range(2):
        starts.append(
            (
                rad.at[p],
                p_send.at[:, y_hi],
                row_send.at[p],
                row_sem.at[y_hi],
                role_device(2 * cuts + p, x_hi, u, core),
            )
        )
    for p in range(2):
        for number_core in range(2):
            starts.append(
                (
                    el_in.at[p],
                    el.at[0, own_slot],
                    init_send.at[p, number_core],
                    el_sem.at[own_slot],
                    role_device(2 * cuts + p, x_hi, u, (core + number_core) % 2),
                )
            )
    for args in starts:
        send(*args)

    for load in loads[4:6]:
        load.wait()
    kr, ki = kx[0], kx[1]
    for number_part, part in enumerate(split(jnp.concatenate([kr, ki], axis=1))):
        k2[number_part] = part
    for half_in in range(2):
        for half_out in range(2):
            block_re = ky[0, half_in * 128 : half_in * 128 + 128, half_out * 128 : half_out * 128 + 128]
            block_im = ky[1, half_in * 128 : half_in * 128 + 128, half_out * 128 : half_out * 128 + 128]
            rows = jnp.concatenate(
                [
                    jnp.concatenate([block_re, block_im], axis=1),
                    jnp.concatenate([-block_im, block_re], axis=1),
                ],
                axis=0,
            )
            for number_part, part in enumerate(split(rows)):
                big_y[
                    number_part,
                    half_in * 256 : half_in * 256 + 256,
                    half_out * 256 : half_out * 256 + 256,
                ] = part

    def gather_copy(step):
        return remote(
            p_send.at[(core + step) % 2],
            field.at[q],
            ag_send.at[step],
            ag_sem.at[step],
            peers[step],
        )

    def sums_copy(step):
        return remote(
            mixed.at[(q + step) % 8], sums.at[q], rs_send.at[step], rs_sem.at[step], peers[step]
        )

    def start_gather():
        for step in range(1, 8):
            gather_copy(step).start()
        field[q] = p_send[core]

    def a_copy(block):
        return remote(
            a_send.at[block], a_recv.at[block], a_ssem.at[block], a_rsem.at[block], beside
        )

    def place_copy(n):
        return remote(
            el.at[n, :, 2:6], el.at[n + 1, :, 2:6], place_send.at[n], place_sem.at[n], ahead
        )

    def state_copy(n, block):
        return remote(
            el.at[n, block, 0:2],
            el.at[n + 1, block, 0:2],
            state_send.at[n, block],
            state_sem.at[n, block],
            ahead,
        )

    def out_electrons(part):
        return (
            el_send.at[part],
            el_back.at[last_number % 2],
            out_send.at[2 + part],
            out_sem.at[2 + last_number % 2],
            home_device(last_number, w, part, u, core),
        )

    def build(n):
        @pl.loop(0, BLOCKS)
        def _(block):
            for row in range(ROWS):
                index_x = el[n, block, 2, row : row + 1, :]
                index_y = el[n, block, 3, row : row + 1, :]
                offset_x = el[n, block, 4, row : row + 1, :]
                offset_y = el[n, block, 5, row : row + 1, :]
                lanes = slice(row * LANES, row * LANES + LANES)
                grid_x = lax.broadcasted_iota(jnp.int32, (256, LANES), 0).astype(f32)
                grid_y = (lax.broadcasted_iota(jnp.int32, (128, LANES), 0) + core * 128).astype(f32)
                weight = jnp.where(grid_x == index_x, 1.0 - offset_x, 0.0) + jnp.where(
                    grid_x == index_x + 1.0, offset_x, 0.0
                )
                hi, lo = split(weight)
                wx[block, 0:256, lanes] = hi
                wx[block, 256:512, lanes] = lo
                wy[block, :, lanes] = jnp.where(
                    grid_y == index_y, 1.0 - offset_y, 0.0
                ) + jnp.where(grid_y == index_y + 1.0, offset_y, 0.0)
            trig[block, 0] = jnp.cos(el[n, block, 0])
            trig[block, 1] = jnp.sin(el[n, block, 0])

    def advance(n, last):
        if not last:
            place_copy(n).start()
        for step in range(1, 8):
            received(field.at[(q + 8 - step) % 8], ag_sem.at[step])
        full = jnp.concatenate([field[owner, part] for owner, part in ROW_BLOCKS], axis=0)
        hi, lo = split(full.T)
        both = jnp.concatenate([hi, lo], axis=0)

        @pl.loop(0, BLOCKS)
        def _(block):
            for row in range(ROWS):
                lanes = slice(row * LANES, row * LANES + LANES)
                first = mm(both, wx[block, 0:256, lanes])
                second = mm(both[0:256], wx[block, 256:512, lanes])
                values = first[0:256] + first[256:512] + second
                weight = wy[block, :, lanes]
                a_send[block, 0, row : row + 1, :] = jnp.sum(
                    values[0:128] * weight, axis=0, keepdims=True
                )
                a_send[block, 1, row : row + 1, :] = jnp.sum(
                    values[128:256] * weight, axis=0, keepdims=True
                )
            a_copy(block).start()

        current[...] = 0.25 * full

        @pl.loop(0, BLOCKS)
        def _(block):
            received(a_recv.at[block], a_rsem.at[block])
            a_re = a_send[block, 0] + a_recv[block, 0]
            a_im = a_send[block, 1] + a_recv[block, 1]
            energy = el[n, block, 1] - coupling * (a_re * trig[block, 0] - a_im * trig[block, 1])
            phase = el[n, block, 0] + phase_step * energy
            el[n, block, 0] = phase
            el[n, block, 1] = energy
            if not last:
                state_copy(n, block).start()
            cos, sin = jnp.cos(phase), jnp.sin(phase)
            for row in range(ROWS):
                lanes = slice(row * LANES, row * LANES + LANES)
                weight = current_gain * wy[block, :, lanes]
                values = jnp.concatenate(
                    [weight * cos[row : row + 1, :], -weight * sin[row : row + 1, :]], axis=0
                )
                hi, lo = split(values)
                v_hi[:, lanes] = hi
                v_lo[:, lanes] = lo
            first = mm_nt(wx[block], v_hi[...])
            second = mm_nt(wx[block, 0:256], v_lo[...])
            current[...] += first[0:256] + first[256:512] + second

        if last:
            for part in range(2):
                el_send[part] = el[n, part * 2 + core, 0:2]
                send(*out_electrons(part))

        total = current[...]
        re, im = total[:, 0:128], total[:, 128:256]
        stacked = jnp.concatenate([total, jnp.concatenate([-im, re], axis=1)], axis=0)
        hi, lo = split(stacked)
        product = mm(k2[0], hi) + mm(k2[1], hi) + mm(k2[0], lo)
        for index, (owner, part) in enumerate(ROW_BLOCKS):
            mixed[owner, part] = product[index * 16 : index * 16 + 16]
        for step in range(1, 8):
            sums_copy(step).start()
        sums[q] = mixed[q]
        if not last:
            received(el.at[n + 1, :, 2:6], place_sem.at[n])

            @pl.loop(0, BLOCKS)
            def _(block):
                received(el.at[n + 1, block, 0:2], state_sem.at[n, block])

            build(n + 1)
        for step in range(1, 8):
            received(sums.at[(q + 8 - step) % 8], rs_sem.at[step])
        halves = [
            ((sums[half] + sums[half + 2]) + (sums[half + 4] + sums[half + 6])).reshape(32, 256)
            for half in range(2)
        ]
        hi, lo = split(jnp.concatenate(halves, axis=1))
        result = mm(hi, big_y[0]) + mm(hi, big_y[1]) + mm(lo, big_y[0])
        result = jnp.where((number + n + 1) % SLICES == 0, 0.0, result)
        for step in range(1, 8):
            gather_copy(step).wait_send()
            sums_copy(step).wait_send()
        if last:
            p_out[...] = jnp.concatenate(
                [result[:, 0:128], result[:, 256:384], result[:, 128:256], result[:, 384:512]],
                axis=1,
            ).reshape(p_out.shape)
        else:
            for half in range(2):
                p_send[half] = result[:, half * 256 : half * 256 + 256].reshape(2, 16, 256)
            start_gather()
            place_copy(n).wait_send()

        @pl.loop(0, BLOCKS)
        def _(block):
            a_copy(block).wait_send()
            if not last:
                state_copy(n, block).wait_send()

    for part in range(2):
        received(p_send.at[:, part], row_sem.at[part])
    start_gather()
    for slot in range(BLOCKS):
        received(el.at[0, slot], el_sem.at[slot])
    build(0)

    @pl.loop(0, ITERS - 1)
    def _(n):
        advance(n, False)

    advance(ITERS - 1, True)

    def out_rows(part):
        return (
            p_out.at[part],
            rad_back.at[row_number % 2],
            out_send.at[part],
            out_sem.at[row_number % 2],
            home_device(row_number, w, part, u, core),
        )

    for part in range(2):
        send(*out_rows(part))
    for args in starts:
        sent(*args)
    for part in range(2):
        sent(*out_rows(part))
        sent(*out_electrons(part))
    for part in range(2):
        received(rad_back.at[part], out_sem.at[part])
        received(el_back.at[part], out_sem.at[2 + part])
    for p in range(2):
        radiation_out[:, p, :] = rad_back[p]
        for row in range(ROWS):
            lanes = slice(row * LANES, row * LANES + LANES)
            for field_number in range(2):
                electrons_out[field_number, p : p + 1, lanes] = el_back[
                    p, field_number, row : row + 1
                ]


def shards(radiation, electrons, cell_index, cell_offset, kernel_x, kernel_y):
    vmem = pl.BlockSpec(memory_space=pltpu.VMEM)
    dma = pltpu.SemaphoreType.DMA
    return pl.pallas_call(
        kernel,
        out_shape=(
            jax.ShapeDtypeStruct(radiation.shape, f32),
            jax.ShapeDtypeStruct(electrons.shape, f32),
        ),
        in_specs=[pl.BlockSpec(memory_space=pltpu.HBM)] * 6,
        out_specs=(vmem, vmem),
        scratch_shapes=[
            pltpu.VMEM(radiation.shape, f32),
            pltpu.VMEM(electrons.shape, f32),
            pltpu.VMEM(cell_index.shape, jnp.int32),
            pltpu.VMEM(cell_offset.shape, f32),
            pltpu.VMEM(kernel_x.shape, f32),
            pltpu.VMEM(kernel_y.shape, f32),
            pltpu.VMEM((2, 2, 16, 256), f32),
            pltpu.VMEM((2, 6, ROWS, LANES), f32),
            pltpu.VMEM((2, 16, 512), f32),
            pltpu.VMEM((2, 2, ROWS, LANES), f32),
            pltpu.VMEM((ITERS, BLOCKS, 6, ROWS, LANES), f32),
            pltpu.VMEM((BLOCKS, 512, ROWS * LANES), bf16),
            pltpu.VMEM((BLOCKS, 128, ROWS * LANES), f32),
            pltpu.VMEM((8, 2, 16, 256), f32),
            pltpu.VMEM((BLOCKS, 2, ROWS, LANES), f32),
            pltpu.VMEM((BLOCKS, 2, ROWS, LANES), f32),
            pltpu.VMEM((BLOCKS, 2, ROWS, LANES), f32),
            pltpu.VMEM((256, ROWS * LANES), bf16),
            pltpu.VMEM((256, ROWS * LANES), bf16),
            pltpu.VMEM((256, 256), f32),
            pltpu.VMEM((2, 256, 512), bf16),
            pltpu.VMEM((2, 512, 512), bf16),
            pltpu.VMEM((8, 2, 16, 256), f32),
            pltpu.VMEM((8, 2, 16, 256), f32),
            pltpu.VMEM((2, 2, 16, 256), f32),
            pltpu.VMEM((2, 16, 512), f32),
            pltpu.VMEM((2, 2, ROWS, LANES), f32),
            dma((2, 2)),
            dma((BLOCKS,)),
            dma((2,)),
            dma((2,)),
            dma((8,)),
            dma((8,)),
            dma((BLOCKS,)),
            dma((BLOCKS,)),
            dma((8,)),
            dma((8,)),
            dma((ITERS,)),
            dma((ITERS,)),
            dma((ITERS, BLOCKS)),
            dma((ITERS, BLOCKS)),
            dma((4,)),
            dma((4,)),
            dma((6,)),
        ],
        compiler_params=pltpu.CompilerParams(
            collective_id=0, has_side_effects=True, vmem_limit_bytes=48 * 1024 * 1024
        ),
    )(radiation, electrons, cell_index, cell_offset, kernel_x, kernel_y)


def solution(mesh):
    placed = (
        P("dom", "cuts", None),
        P(None, "cuts", "dom"),
        P(None, "cuts", "dom"),
        P(None, "cuts", "dom"),
        P(),
        P(),
    )
    return jax.shard_map(
        shards,
        mesh=mesh,
        in_specs=placed,
        out_specs=(P("dom", "cuts", None), P(None, "cuts", "dom")),
        check_vma=False,
    )
```

```python
import jax
import jax.numpy as jnp
from jax import lax
from jax.experimental import pallas as pl
from jax.experimental.pallas import tpu as pltpu
from jax.sharding import PartitionSpec as P

ITERS = 4
SLICES = 16
coupling = 0.5
phase_step = 1.0
current_gain = 1.0
MESH = pl.DeviceIdType.MESH
f32 = jnp.float32
bf16 = jnp.bfloat16
f8 = jnp.float8_e4m3fn

BLOCKS = 4
ROWS = 8
LANES = 256
LOW = 4096.0
PEAK = 32.0
ROW_BLOCKS = [
    ((w * 2 + (t + y_lo) % 2) * 2 + core, t)
    for t in range(2)
    for y_lo in range(2)
    for w in range(2)
    for core in range(2)
]


def split(value):
    hi = value.astype(bf16)
    return hi, (value - hi.astype(f32)).astype(bf16)


def split_low(value):
    hi = value.astype(bf16)
    return hi, ((value - hi.astype(f32)) * LOW).astype(f8)


def mm(a, b):
    return jnp.dot(a, b, preferred_element_type=f32)


def mm_nt(a, b):
    return lax.dot_general(a, b, (((1,), (1,)), ((), ())), preferred_element_type=f32)


def role_device(number, w, u, core):
    pair = number // 2
    x_hi, z = pair // 4, pair % 4
    y_hi = (number % 2 + z) % 2
    x_lo, y_lo = (w + x_hi) % 2, (u + y_hi) % 2
    return x_lo * 4 + z, (y_hi * 2 + y_lo) * 4 + x_hi * 2 + core


def home_device(number, w, t, u, core):
    return number // 2, (t * 2 + (u + t) % 2) * 4 + w * 2 + core


def kernel(
    radiation_hbm,
    electrons_hbm,
    cell_index_hbm,
    cell_offset_hbm,
    kx_hbm,
    ky_hbm,
    radiation_out,
    electrons_out,
    radiation,
    electrons,
    cell_index,
    cell_offset,
    kx,
    ky,
    rad,
    el_in,
    rad_back,
    el_back,
    el,
    wx,
    wy,
    field,
    a_send,
    a_recv,
    trig,
    v_hi,
    v_lo,
    v_top,
    w8,
    current,
    k2,
    big_y,
    mixed,
    sums,
    p_send,
    p_out,
    el_send,
    init_send,
    el_sem,
    row_send,
    row_sem,
    ag_send,
    ag_sem,
    a_ssem,
    a_rsem,
    rs_send,
    rs_sem,
    place_send,
    place_sem,
    state_send,
    state_sem,
    out_send,
    out_sem,
    in_sem,
):
    cuts, dom = lax.axis_index("cuts"), lax.axis_index("dom")
    x_lo, z = cuts // 4, cuts % 4
    y, x_hi, core = dom // 4, dom // 2 % 2, dom % 2
    y_hi = y // 2
    w, u = (x_lo + x_hi) % 2, (y + y_hi) % 2
    number = 2 * (x_hi * 4 + z) + (y_hi + z) % 2
    q = (w * 2 + u) * 2 + core
    last_number = (number + ITERS - 1) % SLICES
    row_number = (number + ITERS) % SLICES

    def peer_device(other):
        return role_device(number, other // 4, other // 2 % 2, other % 2)

    peers = [peer_device((q + step) % 8) for step in range(8)]
    beside = peer_device(q + 1 - 2 * core)
    ahead = role_device((number + SLICES - 1) % SLICES, w, u, core)

    def remote(src, dst, ssem, rsem, device):
        return pltpu.make_async_remote_copy(
            src_ref=src,
            dst_ref=dst,
            send_sem=ssem,
            recv_sem=rsem,
            device_id=device,
            device_id_type=MESH,
        )

    def send(src, dst, ssem, rsem, device):
        self_target = jnp.logical_and(device[0] == cuts, device[1] == dom)

        @pl.when(self_target)
        def _():
            pltpu.make_async_copy(src, dst, rsem).start()

        @pl.when(jnp.logical_not(self_target))
        def _():
            remote(src, dst, ssem, rsem, device).start()

    def sent(src, dst, ssem, rsem, device):
        self_target = jnp.logical_and(device[0] == cuts, device[1] == dom)

        @pl.when(jnp.logical_not(self_target))
        def _():
            remote(src, dst, ssem, rsem, device).wait_send()

    def received(dst, rsem):
        pltpu.make_async_copy(dst, dst, rsem).wait()

    greeted = peers[1:]
    for a in range(2):
        greeted.append(role_device(2 * cuts + a, x_hi, u, core))
        greeted.append(role_device(2 * cuts + a, x_hi, u, 1 - core))
        greeted.append(home_device(number, w, a, u, core))
        greeted.append(home_device(number, w, a, u, 1 - core))
        for moved, end in ((ITERS - 1, last_number), (ITERS, row_number)):
            greeted.append(home_device(end, w, a, u, core))
            greeted.append(role_device((2 * cuts + a + SLICES - moved) % SLICES, x_hi, u, core))
    greeted.append(ahead)
    greeted.append(role_device((number + 1) % SLICES, w, u, core))
    barrier = pltpu.get_barrier_semaphore()
    expected = 0
    for device in greeted:
        others = jnp.logical_or(device[0] != cuts, device[1] != dom)
        expected = expected + others.astype(jnp.int32)

        @pl.when(others)
        def _():
            pl.semaphore_signal(barrier, inc=1, device_id=device, device_id_type=MESH)

    loads = [
        pltpu.make_async_copy(src, dst, in_sem.at[index])
        for index, (src, dst) in enumerate(
            [
                (radiation_hbm, radiation),
                (electrons_hbm, electrons),
                (cell_index_hbm, cell_index),
                (cell_offset_hbm, cell_offset),
                (kx_hbm, kx),
                (ky_hbm, ky),
            ]
        )
    ]
    for load in loads:
        load.start()
    for load in loads[0:4]:
        load.wait()
    for p in range(2):
        for half in range(2):
            for part in range(2):
                column = part * 256 + half * 128
                rad[p, half, :, part * 128 : part * 128 + 128] = radiation[
                    :, p, column : column + 128
                ]
        for row in range(ROWS):
            lanes = slice(row * LANES, row * LANES + LANES)
            for field_number in range(2):
                place = slice(row, row + 1)
                el_in[p, field_number, place] = electrons[field_number, p : p + 1, lanes]
                el_in[p, 2 + field_number, place] = cell_index[
                    field_number, p : p + 1, lanes
                ].astype(f32)
                el_in[p, 4 + field_number, place] = cell_offset[field_number, p : p + 1, lanes]
    pl.semaphore_wait(barrier, expected)

    own_slot = y_hi * 2 + core
    starts = []
    for p in range(2):
        starts.append(
            (
                rad.at[p],
                p_send.at[:, y_hi],
                row_send.at[p],
                row_sem.at[y_hi],
                role_device(2 * cuts + p, x_hi, u, core),
            )
        )
    for p in range(2):
        for number_core in range(2):
            starts.append(
                (
                    el_in.at[p],
                    el.at[0, own_slot],
                    init_send.at[p, number_core],
                    el_sem.at[own_slot],
                    role_device(2 * cuts + p, x_hi, u, (core + number_core) % 2),
                )
            )
    for args in starts:
        send(*args)

    for load in loads[4:6]:
        load.wait()
    kr, ki = kx[0], kx[1]
    for number_part, part in enumerate(split(jnp.concatenate([kr, ki], axis=1))):
        k2[number_part] = part
    for half_in in range(2):
        for half_out in range(2):
            block_re = ky[0, half_in * 128 : half_in * 128 + 128, half_out * 128 : half_out * 128 + 128]
            block_im = ky[1, half_in * 128 : half_in * 128 + 128, half_out * 128 : half_out * 128 + 128]
            rows = jnp.concatenate(
                [
                    jnp.concatenate([block_re, block_im], axis=1),
                    jnp.concatenate([-block_im, block_re], axis=1),
                ],
                axis=0,
            )
            for number_part, part in enumerate(split(rows)):
                big_y[
                    number_part,
                    half_in * 256 : half_in * 256 + 256,
                    half_out * 256 : half_out * 256 + 256,
                ] = part

    def gather_copy(step):
        return remote(
            p_send.at[(core + step) % 2],
            field.at[q],
            ag_send.at[step],
            ag_sem.at[step],
            peers[step],
        )

    def sums_copy(step):
        return remote(
            mixed.at[(q + step) % 8], sums.at[q], rs_send.at[step], rs_sem.at[step], peers[step]
        )

    def start_gather():
        for step in range(1, 8):
            gather_copy(step).start()
        field[q] = p_send[core]

    def a_copy(block):
        return remote(
            a_send.at[block], a_recv.at[block], a_ssem.at[block], a_rsem.at[block], beside
        )

    def place_copy(n):
        return remote(
            el.at[n, :, 2:6], el.at[n + 1, :, 2:6], place_send.at[n], place_sem.at[n], ahead
        )

    def state_copy(n, block):
        return remote(
            el.at[n, block, 0:2],
            el.at[n + 1, block, 0:2],
            state_send.at[n, block],
            state_sem.at[n, block],
            ahead,
        )

    def out_electrons(part):
        return (
            el_send.at[part],
            el_back.at[last_number % 2],
            out_send.at[2 + part],
            out_sem.at[2 + last_number % 2],
            home_device(last_number, w, part, u, core),
        )

    def build(n):
        @pl.loop(0, BLOCKS)
        def _(block):
            for row in range(ROWS):
                index_x = el[n, block, 2, row : row + 1, :]
                index_y = el[n, block, 3, row : row + 1, :]
                offset_x = el[n, block, 4, row : row + 1, :]
                offset_y = el[n, block, 5, row : row + 1, :]
                lanes = slice(row * LANES, row * LANES + LANES)
                grid_x = lax.broadcasted_iota(jnp.int32, (256, LANES), 0).astype(f32)
                grid_y = (lax.broadcasted_iota(jnp.int32, (128, LANES), 0) + core * 128).astype(f32)
                weight = jnp.where(grid_x == index_x, 1.0 - offset_x, 0.0) + jnp.where(
                    grid_x == index_x + 1.0, offset_x, 0.0
                )
                hi, lo = split_low(weight)
                wx[block, 0:256, lanes] = hi
                w8[block, 0:256, lanes] = weight.astype(f8)
                w8[block, 256:512, lanes] = lo
                wy[block, :, lanes] = jnp.where(
                    grid_y == index_y, 1.0 - offset_y, 0.0
                ) + jnp.where(grid_y == index_y + 1.0, offset_y, 0.0)
            trig[block, 0] = jnp.cos(el[n, block, 0])
            trig[block, 1] = jnp.sin(el[n, block, 0])

    def advance(n, last):
        if not last:
            place_copy(n).start()
        for step in range(1, 8):
            received(field.at[(q + 8 - step) % 8], ag_sem.at[step])
        full = jnp.concatenate([field[owner, part] for owner, part in ROW_BLOCKS], axis=0)
        turned = full.T
        peak = jnp.max(jnp.max(jnp.abs(turned), axis=0, keepdims=True), axis=1, keepdims=True)
        peak = jnp.maximum(peak, 1e-30)
        scaled = turned * (PEAK / peak)
        hi, lo = split_low(scaled)
        low = jnp.concatenate([lo, scaled.astype(f8)], axis=1)
        unscale = jnp.broadcast_to(peak * (1.0 / PEAK), (1, LANES))

        @pl.loop(0, BLOCKS)
        def _(block):
            for row in range(ROWS):
                lanes = slice(row * LANES, row * LANES + LANES)
                values = mm(hi, wx[block, :, lanes]) + mm(low, w8[block, :, lanes]) * (1.0 / LOW)
                weight = wy[block, :, lanes]
                a_send[block, 0, row : row + 1, :] = unscale * jnp.sum(
                    values[0:128] * weight, axis=0, keepdims=True
                )
                a_send[block, 1, row : row + 1, :] = unscale * jnp.sum(
                    values[128:256] * weight, axis=0, keepdims=True
                )
            a_copy(block).start()

        current[...] = 0.25 * full

        @pl.loop(0, BLOCKS)
        def _(block):
            received(a_recv.at[block], a_rsem.at[block])
            a_re = a_send[block, 0] + a_recv[block, 0]
            a_im = a_send[block, 1] + a_recv[block, 1]
            energy = el[n, block, 1] - coupling * (a_re * trig[block, 0] - a_im * trig[block, 1])
            phase = el[n, block, 0] + phase_step * energy
            el[n, block, 0] = phase
            el[n, block, 1] = energy
            if not last:
                state_copy(n, block).start()
            cos, sin = jnp.cos(phase), jnp.sin(phase)
            for row in range(ROWS):
                lanes = slice(row * LANES, row * LANES + LANES)
                weight = current_gain * wy[block, :, lanes]
                values = jnp.concatenate(
                    [weight * cos[row : row + 1, :], -weight * sin[row : row + 1, :]], axis=0
                )
                hi, lo = split_low(values)
                v_hi[:, lanes] = hi
                v_lo[:, lanes] = lo
                v_top[:, lanes] = values.astype(f8)
            current[...] += mm_nt(wx[block], v_hi[...]) + (
                mm_nt(w8[block, 0:256], v_lo[...]) + mm_nt(w8[block, 256:512], v_top[...])
            ) * (1.0 / LOW)

        if last:
            for part in range(2):
                el_send[part] = el[n, part * 2 + core, 0:2]
                send(*out_electrons(part))

        total = current[...]
        re, im = total[:, 0:128], total[:, 128:256]
        stacked = jnp.concatenate([total, jnp.concatenate([-im, re], axis=1)], axis=0)
        hi, lo = split(stacked)
        product = mm(k2[0], hi) + mm(k2[1], hi) + mm(k2[0], lo)
        for index, (owner, part) in enumerate(ROW_BLOCKS):
            mixed[owner, part] = product[index * 16 : index * 16 + 16]
        for step in range(1, 8):
            sums_copy(step).start()
        sums[q] = mixed[q]
        if not last:
            received(el.at[n + 1, :, 2:6], place_sem.at[n])

            @pl.loop(0, BLOCKS)
            def _(block):
                received(el.at[n + 1, block, 0:2], state_sem.at[n, block])

            build(n + 1)
        for step in range(1, 8):
            received(sums.at[(q + 8 - step) % 8], rs_sem.at[step])
        halves = [
            ((sums[half] + sums[half + 2]) + (sums[half + 4] + sums[half + 6])).reshape(32, 256)
            for half in range(2)
        ]
        hi, lo = split(jnp.concatenate(halves, axis=1))
        result = mm(hi, big_y[0]) + mm(hi, big_y[1]) + mm(lo, big_y[0])
        result = jnp.where((number + n + 1) % SLICES == 0, 0.0, result)
        for step in range(1, 8):
            gather_copy(step).wait_send()
            sums_copy(step).wait_send()
        if last:
            p_out[...] = jnp.concatenate(
                [result[:, 0:128], result[:, 256:384], result[:, 128:256], result[:, 384:512]],
                axis=1,
            ).reshape(p_out.shape)
        else:
            for half in range(2):
                p_send[half] = result[:, half * 256 : half * 256 + 256].reshape(2, 16, 256)
            start_gather()
            place_copy(n).wait_send()

        @pl.loop(0, BLOCKS)
        def _(block):
            a_copy(block).wait_send()
            if not last:
                state_copy(n, block).wait_send()

    for part in range(2):
        received(p_send.at[:, part], row_sem.at[part])
    start_gather()
    for slot in range(BLOCKS):
        received(el.at[0, slot], el_sem.at[slot])
    build(0)

    @pl.loop(0, ITERS - 1)
    def _(n):
        advance(n, False)

    advance(ITERS - 1, True)

    def out_rows(part):
        return (
            p_out.at[part],
            rad_back.at[row_number % 2],
            out_send.at[part],
            out_sem.at[row_number % 2],
            home_device(row_number, w, part, u, core),
        )

    for part in range(2):
        send(*out_rows(part))
    for args in starts:
        sent(*args)
    for part in range(2):
        sent(*out_rows(part))
        sent(*out_electrons(part))
    for part in range(2):
        received(rad_back.at[part], out_sem.at[part])
        received(el_back.at[part], out_sem.at[2 + part])
    for p in range(2):
        radiation_out[:, p, :] = rad_back[p]
        for row in range(ROWS):
            lanes = slice(row * LANES, row * LANES + LANES)
            for field_number in range(2):
                electrons_out[field_number, p : p + 1, lanes] = el_back[
                    p, field_number, row : row + 1
                ]


def shards(radiation, electrons, cell_index, cell_offset, kernel_x, kernel_y):
    vmem = pl.BlockSpec(memory_space=pltpu.VMEM)
    dma = pltpu.SemaphoreType.DMA
    return pl.pallas_call(
        kernel,
        out_shape=(
            jax.ShapeDtypeStruct(radiation.shape, f32),
            jax.ShapeDtypeStruct(electrons.shape, f32),
        ),
        in_specs=[pl.BlockSpec(memory_space=pltpu.HBM)] * 6,
        out_specs=(vmem, vmem),
        scratch_shapes=[
            pltpu.VMEM(radiation.shape, f32),
            pltpu.VMEM(electrons.shape, f32),
            pltpu.VMEM(cell_index.shape, jnp.int32),
            pltpu.VMEM(cell_offset.shape, f32),
            pltpu.VMEM(kernel_x.shape, f32),
            pltpu.VMEM(kernel_y.shape, f32),
            pltpu.VMEM((2, 2, 16, 256), f32),
            pltpu.VMEM((2, 6, ROWS, LANES), f32),
            pltpu.VMEM((2, 16, 512), f32),
            pltpu.VMEM((2, 2, ROWS, LANES), f32),
            pltpu.VMEM((ITERS, BLOCKS, 6, ROWS, LANES), f32),
            pltpu.VMEM((BLOCKS, 256, ROWS * LANES), bf16),
            pltpu.VMEM((BLOCKS, 128, ROWS * LANES), f32),
            pltpu.VMEM((8, 2, 16, 256), f32),
            pltpu.VMEM((BLOCKS, 2, ROWS, LANES), f32),
            pltpu.VMEM((BLOCKS, 2, ROWS, LANES), f32),
            pltpu.VMEM((BLOCKS, 2, ROWS, LANES), f32),
            pltpu.VMEM((256, ROWS * LANES), bf16),
            pltpu.VMEM((256, ROWS * LANES), f8),
            pltpu.VMEM((256, ROWS * LANES), f8),
            pltpu.VMEM((BLOCKS, 512, ROWS * LANES), f8),
            pltpu.VMEM((256, 256), f32),
            pltpu.VMEM((2, 256, 512), bf16),
            pltpu.VMEM((2, 512, 512), bf16),
            pltpu.VMEM((8, 2, 16, 256), f32),
            pltpu.VMEM((8, 2, 16, 256), f32),
            pltpu.VMEM((2, 2, 16, 256), f32),
            pltpu.VMEM((2, 16, 512), f32),
            pltpu.VMEM((2, 2, ROWS, LANES), f32),
            dma((2, 2)),
            dma((BLOCKS,)),
            dma((2,)),
            dma((2,)),
            dma((8,)),
            dma((8,)),
            dma((BLOCKS,)),
            dma((BLOCKS,)),
            dma((8,)),
            dma((8,)),
            dma((ITERS,)),
            dma((ITERS,)),
            dma((ITERS, BLOCKS)),
            dma((ITERS, BLOCKS)),
            dma((4,)),
            dma((4,)),
            dma((6,)),
        ],
        compiler_params=pltpu.CompilerParams(
            collective_id=0, has_side_effects=True, vmem_limit_bytes=63 * 1024 * 1024
        ),
    )(radiation, electrons, cell_index, cell_offset, kernel_x, kernel_y)


def solution(mesh):
    placed = (
        P("dom", "cuts", None),
        P(None, "cuts", "dom"),
        P(None, "cuts", "dom"),
        P(None, "cuts", "dom"),
        P(),
        P(),
    )
    return jax.shard_map(
        shards,
        mesh=mesh,
        in_specs=placed,
        out_specs=(P("dom", "cuts", None), P(None, "cuts", "dom")),
        check_vma=False,
    )
```

```python
import jax
import jax.numpy as jnp
from jax import lax
from jax.experimental import pallas as pl
from jax.experimental.pallas import tpu as pltpu
from jax.sharding import PartitionSpec as P

ITERS = 4
SLICES = 16
coupling = 0.5
phase_step = 1.0
current_gain = 1.0
MESH = pl.DeviceIdType.MESH
f32 = jnp.float32
bf16 = jnp.bfloat16
f8 = jnp.float8_e4m3fn

BLOCKS = 4
ROWS = 8
LANES = 256
SEND_ORDER = (6, 7, 2, 3, 4, 5, 1)
LOW = 4096.0
PEAK = 32.0
ROW_BLOCKS = [
    ((w * 2 + (t + y_lo) % 2) * 2 + core, t)
    for t in range(2)
    for y_lo in range(2)
    for w in range(2)
    for core in range(2)
]


def split(value):
    hi = value.astype(bf16)
    return hi, (value - hi.astype(f32)).astype(bf16)


def split_low(value):
    hi = value.astype(bf16)
    return hi, ((value - hi.astype(f32)) * LOW).astype(f8)


def mm(a, b):
    return jnp.dot(a, b, preferred_element_type=f32)


def mm_nt(a, b):
    return lax.dot_general(a, b, (((1,), (1,)), ((), ())), preferred_element_type=f32)


def role_device(number, w, u, core):
    pair = number // 2
    x_hi, z = pair // 4, pair % 4
    y_hi = (number % 2 + z) % 2
    x_lo, y_lo = (w + x_hi) % 2, (u + y_hi) % 2
    return x_lo * 4 + z, (y_hi * 2 + y_lo) * 4 + x_hi * 2 + core


def home_device(number, w, t, u, core):
    return number // 2, (t * 2 + (u + t) % 2) * 4 + w * 2 + core


def kernel(
    radiation_hbm,
    electrons_hbm,
    cell_index_hbm,
    cell_offset_hbm,
    kx_hbm,
    ky_hbm,
    radiation_out,
    electrons_out,
    radiation,
    electrons,
    cell_index,
    cell_offset,
    kx,
    ky,
    rad,
    el_in,
    rad_back,
    el_back,
    el,
    wx,
    wy,
    field,
    a_send,
    a_recv,
    trig,
    v_hi,
    v_lo,
    v_top,
    w8,
    current,
    k2,
    big_y,
    mixed,
    sums,
    p_send,
    p_out,
    el_send,
    init_send,
    el_sem,
    row_send,
    row_sem,
    ag_send,
    ag_sem,
    a_ssem,
    a_rsem,
    rs_send,
    rs_sem,
    place_send,
    place_sem,
    state_send,
    state_sem,
    out_send,
    out_sem,
    in_sem,
):
    cuts, dom = lax.axis_index("cuts"), lax.axis_index("dom")
    x_lo, z = cuts // 4, cuts % 4
    y, x_hi, core = dom // 4, dom // 2 % 2, dom % 2
    y_hi = y // 2
    w, u = (x_lo + x_hi) % 2, (y + y_hi) % 2
    number = 2 * (x_hi * 4 + z) + (y_hi + z) % 2
    q = (w * 2 + u) * 2 + core
    last_number = (number + ITERS - 1) % SLICES
    row_number = (number + ITERS) % SLICES

    def peer_device(other):
        return role_device(number, other // 4, other // 2 % 2, other % 2)

    owners = [
        ((w + key // 4) % 2 * 2 + (u + key // 2) % 2) * 2 + (core + key) % 2 for key in range(8)
    ]
    peers = [peer_device(owner) for owner in owners]
    beside = peers[1]
    ahead = role_device((number + SLICES - 1) % SLICES, w, u, core)

    def remote(src, dst, ssem, rsem, device):
        return pltpu.make_async_remote_copy(
            src_ref=src,
            dst_ref=dst,
            send_sem=ssem,
            recv_sem=rsem,
            device_id=device,
            device_id_type=MESH,
        )

    def send(src, dst, ssem, rsem, device):
        self_target = jnp.logical_and(device[0] == cuts, device[1] == dom)

        @pl.when(self_target)
        def _():
            pltpu.make_async_copy(src, dst, rsem).start()

        @pl.when(jnp.logical_not(self_target))
        def _():
            remote(src, dst, ssem, rsem, device).start()

    def sent(src, dst, ssem, rsem, device):
        self_target = jnp.logical_and(device[0] == cuts, device[1] == dom)

        @pl.when(jnp.logical_not(self_target))
        def _():
            remote(src, dst, ssem, rsem, device).wait_send()

    def received(dst, rsem):
        pltpu.make_async_copy(dst, dst, rsem).wait()

    greeted = peers[1:]
    for a in range(2):
        greeted.append(role_device(2 * cuts + a, x_hi, u, core))
        greeted.append(role_device(2 * cuts + a, x_hi, u, 1 - core))
        greeted.append(home_device(number, w, a, u, core))
        greeted.append(home_device(number, w, a, u, 1 - core))
        for moved, end in ((ITERS - 1, last_number), (ITERS, row_number)):
            greeted.append(home_device(end, w, a, u, core))
            greeted.append(role_device((2 * cuts + a + SLICES - moved) % SLICES, x_hi, u, core))
    greeted.append(ahead)
    greeted.append(role_device((number + 1) % SLICES, w, u, core))
    barrier = pltpu.get_barrier_semaphore()
    expected = 0
    for device in greeted:
        others = jnp.logical_or(device[0] != cuts, device[1] != dom)
        expected = expected + others.astype(jnp.int32)

        @pl.when(others)
        def _():
            pl.semaphore_signal(barrier, inc=1, device_id=device, device_id_type=MESH)

    loads = [
        pltpu.make_async_copy(src, dst, in_sem.at[index])
        for index, (src, dst) in enumerate(
            [
                (radiation_hbm, radiation),
                (electrons_hbm, electrons),
                (cell_index_hbm, cell_index),
                (cell_offset_hbm, cell_offset),
                (kx_hbm, kx),
                (ky_hbm, ky),
            ]
        )
    ]
    for load in loads:
        load.start()
    for load in loads[0:4]:
        load.wait()
    for p in range(2):
        for half in range(2):
            for part in range(2):
                column = part * 256 + half * 128
                rad[p, half, :, part * 128 : part * 128 + 128] = radiation[
                    :, p, column : column + 128
                ]
        for row in range(ROWS):
            lanes = slice(row * LANES, row * LANES + LANES)
            for field_number in range(2):
                place = slice(row, row + 1)
                el_in[p, field_number, place] = electrons[field_number, p : p + 1, lanes]
                el_in[p, 2 + field_number, place] = cell_index[
                    field_number, p : p + 1, lanes
                ].astype(f32)
                el_in[p, 4 + field_number, place] = cell_offset[field_number, p : p + 1, lanes]
    pl.semaphore_wait(barrier, expected)

    own_slot = y_hi * 2 + core
    starts = []
    for p in range(2):
        starts.append(
            (
                rad.at[p],
                p_send.at[:, y_hi],
                row_send.at[p],
                row_sem.at[y_hi],
                role_device(2 * cuts + p, x_hi, u, core),
            )
        )
    for p in range(2):
        for number_core in range(2):
            starts.append(
                (
                    el_in.at[p],
                    el.at[0, own_slot],
                    init_send.at[p, number_core],
                    el_sem.at[own_slot],
                    role_device(2 * cuts + p, x_hi, u, (core + number_core) % 2),
                )
            )
    for args in starts:
        send(*args)

    for load in loads[4:6]:
        load.wait()
    kr, ki = kx[0], kx[1]
    for number_part, part in enumerate(split(jnp.concatenate([kr, ki], axis=1))):
        k2[number_part * 256 : number_part * 256 + 256] = part
    for half_in in range(2):
        for half_out in range(2):
            block_re = ky[0, half_in * 128 : half_in * 128 + 128, half_out * 128 : half_out * 128 + 128]
            block_im = ky[1, half_in * 128 : half_in * 128 + 128, half_out * 128 : half_out * 128 + 128]
            rows = jnp.concatenate(
                [
                    jnp.concatenate([block_re, block_im], axis=1),
                    jnp.concatenate([-block_im, block_re], axis=1),
                ],
                axis=0,
            )
            for number_part, part in enumerate(split(rows)):
                big_y[
                    number_part,
                    half_in * 256 : half_in * 256 + 256,
                    half_out * 256 : half_out * 256 + 256,
                ] = part

    def gather_copy(step):
        return remote(
            p_send.at[(core + step) % 2],
            field.at[q],
            ag_send.at[step],
            ag_sem.at[step],
            peers[step],
        )

    def sums_copy(step):
        return remote(
            mixed.at[owners[step]], sums.at[q], rs_send.at[step], rs_sem.at[step], peers[step]
        )

    def start_gather():
        for step in SEND_ORDER:
            gather_copy(step).start()
        field[q] = p_send[core]

    def a_copy(block):
        return remote(
            a_send.at[block], a_recv.at[block], a_ssem.at[block], a_rsem.at[block], beside
        )

    def place_copy(n):
        return remote(
            el.at[n, :, 2:6], el.at[n + 1, :, 2:6], place_send.at[n], place_sem.at[n], ahead
        )

    def state_copy(n, block):
        return remote(
            el.at[n, block, 0:2],
            el.at[n + 1, block, 0:2],
            state_send.at[n, block],
            state_sem.at[n, block],
            ahead,
        )

    def out_electrons(part):
        return (
            el_send.at[part],
            el_back.at[last_number % 2],
            out_send.at[2 + part],
            out_sem.at[2 + last_number % 2],
            home_device(last_number, w, part, u, core),
        )

    def out_rows(part):
        return (
            p_out.at[part],
            rad_back.at[row_number % 2],
            out_send.at[part],
            out_sem.at[row_number % 2],
            home_device(row_number, w, part, u, core),
        )

    def build(n):
        @pl.loop(0, BLOCKS)
        def _(block):
            for row in range(ROWS):
                index_x = el[n, block, 2, row : row + 1, :]
                index_y = el[n, block, 3, row : row + 1, :]
                offset_x = el[n, block, 4, row : row + 1, :]
                offset_y = el[n, block, 5, row : row + 1, :]
                lanes = slice(row * LANES, row * LANES + LANES)
                grid_x = lax.broadcasted_iota(jnp.int32, (256, LANES), 0).astype(f32)
                grid_y = (lax.broadcasted_iota(jnp.int32, (128, LANES), 0) + core * 128).astype(f32)
                weight = jnp.where(grid_x == index_x, 1.0 - offset_x, 0.0) + jnp.where(
                    grid_x == index_x + 1.0, offset_x, 0.0
                )
                hi, lo = split_low(weight)
                wx[block, 0:256, lanes] = hi
                w8[block, 0:256, lanes] = weight.astype(f8)
                w8[block, 256:512, lanes] = lo
                wy[block, :, lanes] = jnp.where(
                    grid_y == index_y, 1.0 - offset_y, 0.0
                ) + jnp.where(grid_y == index_y + 1.0, offset_y, 0.0)
            trig[block, 0] = jnp.cos(el[n, block, 0])
            trig[block, 1] = jnp.sin(el[n, block, 0])

    def advance(n, last):
        if not last:
            place_copy(n).start()
        for step in SEND_ORDER:
            received(field.at[owners[step]], ag_sem.at[step])
        full = jnp.concatenate([field[owner, part] for owner, part in ROW_BLOCKS], axis=0)
        turned = full.T
        peak = jnp.max(jnp.max(jnp.abs(turned), axis=0, keepdims=True), axis=1, keepdims=True)
        peak = jnp.maximum(peak, 1e-30)
        scaled = turned * (PEAK / peak)
        hi, lo = split_low(scaled)
        low = jnp.concatenate([lo, scaled.astype(f8)], axis=1)
        unscale = jnp.broadcast_to(peak * (1.0 / PEAK), (1, LANES))

        @pl.loop(0, BLOCKS)
        def _(block):
            for row in range(ROWS):
                lanes = slice(row * LANES, row * LANES + LANES)
                values = mm(hi, wx[block, :, lanes]) + mm(low, w8[block, :, lanes]) * (1.0 / LOW)
                weight = wy[block, :, lanes]
                a_send[block, 0, row : row + 1, :] = unscale * jnp.sum(
                    values[0:128] * weight, axis=0, keepdims=True
                )
                a_send[block, 1, row : row + 1, :] = unscale * jnp.sum(
                    values[128:256] * weight, axis=0, keepdims=True
                )
            a_copy(block).start()

        current[...] = 0.25 * full

        @pl.loop(0, BLOCKS)
        def _(block):
            received(a_recv.at[block], a_rsem.at[block])
            a_re = a_send[block, 0] + a_recv[block, 0]
            a_im = a_send[block, 1] + a_recv[block, 1]
            energy = el[n, block, 1] - coupling * (a_re * trig[block, 0] - a_im * trig[block, 1])
            phase = el[n, block, 0] + phase_step * energy
            el[n, block, 0] = phase
            el[n, block, 1] = energy
            if not last:
                state_copy(n, block).start()
            cos, sin = jnp.cos(phase), jnp.sin(phase)
            for row in range(ROWS):
                lanes = slice(row * LANES, row * LANES + LANES)
                weight = current_gain * wy[block, :, lanes]
                values = jnp.concatenate(
                    [weight * cos[row : row + 1, :], -weight * sin[row : row + 1, :]], axis=0
                )
                hi, lo = split_low(values)
                v_hi[:, lanes] = hi
                v_lo[:, lanes] = lo
                v_top[:, lanes] = values.astype(f8)
            current[...] += mm_nt(wx[block], v_hi[...]) + (
                mm_nt(w8[block, 0:256], v_lo[...]) + mm_nt(w8[block, 256:512], v_top[...])
            ) * (1.0 / LOW)

        if last:
            for part in range(2):
                el_send[part] = el[n, part * 2 + core, 0:2]
                send(*out_electrons(part))

        total = current[...]
        re, im = total[:, 0:128], total[:, 128:256]
        stacked = jnp.concatenate([total, jnp.concatenate([-im, re], axis=1)], axis=0)
        hi, lo = split(stacked)
        product = mm(k2[...], hi)
        product = product[0:256] + product[256:512] + mm(k2[0:256], lo)
        for index, (owner, part) in enumerate(ROW_BLOCKS):
            mixed[owner, part] = product[index * 16 : index * 16 + 16]
        for step in SEND_ORDER:
            sums_copy(step).start()
        sums[q] = mixed[q]
        for step in SEND_ORDER:
            gather_copy(step).wait_send()
        if not last:
            received(el.at[n + 1, :, 2:6], place_sem.at[n])

            @pl.loop(0, BLOCKS)
            def _(block):
                received(el.at[n + 1, block, 0:2], state_sem.at[n, block])

            build(n + 1)
        for step in SEND_ORDER:
            received(sums.at[owners[step]], rs_sem.at[step])
        halves = [
            ((sums[half] + sums[half + 2]) + (sums[half + 4] + sums[half + 6])).reshape(32, 256)
            for half in range(2)
        ]
        hi, lo = split(jnp.concatenate(halves, axis=1))
        result = mm(jnp.concatenate([hi, lo], axis=0), big_y[0])
        result = result[0:32] + result[32:64] + mm(hi, big_y[1])
        result = jnp.where((number + n + 1) % SLICES == 0, 0.0, result)
        if last:
            p_out[...] = jnp.concatenate(
                [result[:, 0:128], result[:, 256:384], result[:, 128:256], result[:, 384:512]],
                axis=1,
            ).reshape(p_out.shape)
            for part in range(2):
                send(*out_rows(part))
        else:
            for half in range(2):
                p_send[half] = result[:, half * 256 : half * 256 + 256].reshape(2, 16, 256)
            start_gather()
            place_copy(n).wait_send()

        for step in SEND_ORDER:
            sums_copy(step).wait_send()
        for block in range(BLOCKS):
            a_copy(block).wait_send()
            if not last:
                state_copy(n, block).wait_send()

    for part in range(2):
        received(p_send.at[:, part], row_sem.at[part])
    start_gather()
    for slot in range(BLOCKS):
        received(el.at[0, slot], el_sem.at[slot])
    build(0)

    @pl.loop(0, ITERS - 1)
    def _(n):
        advance(n, False)

    advance(ITERS - 1, True)

    for args in starts:
        sent(*args)
    for part in range(2):
        sent(*out_rows(part))
        sent(*out_electrons(part))
    for part in range(2):
        received(rad_back.at[part], out_sem.at[part])
        received(el_back.at[part], out_sem.at[2 + part])
    for p in range(2):
        radiation_out[:, p, :] = rad_back[p]
        for row in range(ROWS):
            lanes = slice(row * LANES, row * LANES + LANES)
            for field_number in range(2):
                electrons_out[field_number, p : p + 1, lanes] = el_back[
                    p, field_number, row : row + 1
                ]


def shards(radiation, electrons, cell_index, cell_offset, kernel_x, kernel_y):
    vmem = pl.BlockSpec(memory_space=pltpu.VMEM)
    dma = pltpu.SemaphoreType.DMA
    return pl.pallas_call(
        kernel,
        out_shape=(
            jax.ShapeDtypeStruct(radiation.shape, f32),
            jax.ShapeDtypeStruct(electrons.shape, f32),
        ),
        in_specs=[pl.BlockSpec(memory_space=pltpu.HBM)] * 6,
        out_specs=(vmem, vmem),
        scratch_shapes=[
            pltpu.VMEM(radiation.shape, f32),
            pltpu.VMEM(electrons.shape, f32),
            pltpu.VMEM(cell_index.shape, jnp.int32),
            pltpu.VMEM(cell_offset.shape, f32),
            pltpu.VMEM(kernel_x.shape, f32),
            pltpu.VMEM(kernel_y.shape, f32),
            pltpu.VMEM((2, 2, 16, 256), f32),
            pltpu.VMEM((2, 6, ROWS, LANES), f32),
            pltpu.VMEM((2, 16, 512), f32),
            pltpu.VMEM((2, 2, ROWS, LANES), f32),
            pltpu.VMEM((ITERS, BLOCKS, 6, ROWS, LANES), f32),
            pltpu.VMEM((BLOCKS, 256, ROWS * LANES), bf16),
            pltpu.VMEM((BLOCKS, 128, ROWS * LANES), f32),
            pltpu.VMEM((8, 2, 16, 256), f32),
            pltpu.VMEM((BLOCKS, 2, ROWS, LANES), f32),
            pltpu.VMEM((BLOCKS, 2, ROWS, LANES), f32),
            pltpu.VMEM((BLOCKS, 2, ROWS, LANES), f32),
            pltpu.VMEM((256, ROWS * LANES), bf16),
            pltpu.VMEM((256, ROWS * LANES), f8),
            pltpu.VMEM((256, ROWS * LANES), f8),
            pltpu.VMEM((BLOCKS, 512, ROWS * LANES), f8),
            pltpu.VMEM((256, 256), f32),
            pltpu.VMEM((512, 512), bf16),
            pltpu.VMEM((2, 512, 512), bf16),
            pltpu.VMEM((8, 2, 16, 256), f32),
            pltpu.VMEM((8, 2, 16, 256), f32),
            pltpu.VMEM((2, 2, 16, 256), f32),
            pltpu.VMEM((2, 16, 512), f32),
            pltpu.VMEM((2, 2, ROWS, LANES), f32),
            dma((2, 2)),
            dma((BLOCKS,)),
            dma((2,)),
            dma((2,)),
            dma((8,)),
            dma((8,)),
            dma((BLOCKS,)),
            dma((BLOCKS,)),
            dma((8,)),
            dma((8,)),
            dma((ITERS,)),
            dma((ITERS,)),
            dma((ITERS, BLOCKS)),
            dma((ITERS, BLOCKS)),
            dma((4,)),
            dma((4,)),
            dma((6,)),
        ],
        compiler_params=pltpu.CompilerParams(
            collective_id=0, has_side_effects=True, vmem_limit_bytes=63 * 1024 * 1024
        ),
    )(radiation, electrons, cell_index, cell_offset, kernel_x, kernel_y)


def solution(mesh):
    placed = (
        P("dom", "cuts", None),
        P(None, "cuts", "dom"),
        P(None, "cuts", "dom"),
        P(None, "cuts", "dom"),
        P(),
        P(),
    )
    return jax.shard_map(
        shards,
        mesh=mesh,
        in_specs=placed,
        out_specs=(P("dom", "cuts", None), P(None, "cuts", "dom")),
        check_vma=False,
    )
```

```python
import jax
import jax.numpy as jnp
from jax import lax
from jax.experimental import pallas as pl
from jax.experimental.pallas import tpu as pltpu
from jax.sharding import PartitionSpec as P

ITERS = 4
SLICES = 16
coupling = 0.5
phase_step = 1.0
current_gain = 1.0
MESH = pl.DeviceIdType.MESH
f32 = jnp.float32
bf16 = jnp.bfloat16
f8 = jnp.float8_e4m3fn

BLOCKS = 4
ROWS = 8
LANES = 256
SEND_ORDER = (6, 7, 2, 3, 4, 5, 1)
LOW = 4096.0
PEAK = 32.0
ROW_BLOCKS = [
    ((w * 2 + (t + y_lo) % 2) * 2 + core, t)
    for t in range(2)
    for y_lo in range(2)
    for w in range(2)
    for core in range(2)
]


def split(value, scale=1.0):
    hi = value.astype(bf16)
    return hi, ((value - hi.astype(f32)) * scale).astype(bf16)


def split_low(value):
    hi = value.astype(bf16)
    return hi, ((value - hi.astype(f32)) * LOW).astype(f8)


def mm(a, b):
    return jnp.dot(a, b, preferred_element_type=f32)


def mm_nt(a, b):
    return lax.dot_general(a, b, (((1,), (1,)), ((), ())), preferred_element_type=f32)


def role_device(number, w, u, core):
    pair = number // 2
    x_hi, z = pair // 4, pair % 4
    y_hi = (number % 2 + z) % 2
    x_lo, y_lo = (w + x_hi) % 2, (u + y_hi) % 2
    return x_lo * 4 + z, (y_hi * 2 + y_lo) * 4 + x_hi * 2 + core


def home_device(number, w, t, u, core):
    return number // 2, (t * 2 + (u + t) % 2) * 4 + w * 2 + core


def kernel(
    radiation_hbm,
    electrons_hbm,
    cell_index_hbm,
    cell_offset_hbm,
    kx_hbm,
    ky_hbm,
    radiation_out,
    electrons_out,
    radiation,
    electrons,
    cell_index,
    cell_offset,
    kx,
    ky,
    rad,
    el_in,
    rad_back,
    el_back,
    el,
    wx,
    wy,
    field,
    a_send,
    a_recv,
    trig,
    v_hi,
    v_lo,
    v_top,
    w8,
    current,
    k2,
    big_y,
    mixed,
    sums,
    p_send,
    p_out,
    el_send,
    init_send,
    el_sem,
    row_send,
    row_sem,
    ag_send,
    ag_sem,
    a_ssem,
    a_rsem,
    rs_send,
    rs_sem,
    place_send,
    place_sem,
    state_send,
    state_sem,
    out_send,
    out_sem,
    in_sem,
):
    cuts, dom = lax.axis_index("cuts"), lax.axis_index("dom")
    x_lo, z = cuts // 4, cuts % 4
    y, x_hi, core = dom // 4, dom // 2 % 2, dom % 2
    y_hi = y // 2
    w, u = (x_lo + x_hi) % 2, (y + y_hi) % 2
    number = 2 * (x_hi * 4 + z) + (y_hi + z) % 2
    q = (w * 2 + u) * 2 + core
    last_number = (number + ITERS - 1) % SLICES
    row_number = (number + ITERS) % SLICES

    def peer_device(other):
        return role_device(number, other // 4, other // 2 % 2, other % 2)

    owners = [
        ((w + key // 4) % 2 * 2 + (u + key // 2) % 2) * 2 + (core + key) % 2 for key in range(8)
    ]
    peers = [peer_device(owner) for owner in owners]
    beside = peers[1]
    ahead = role_device((number + SLICES - 1) % SLICES, w, u, core)

    def remote(src, dst, ssem, rsem, device):
        return pltpu.make_async_remote_copy(
            src_ref=src,
            dst_ref=dst,
            send_sem=ssem,
            recv_sem=rsem,
            device_id=device,
            device_id_type=MESH,
        )

    def send(src, dst, ssem, rsem, device):
        self_target = jnp.logical_and(device[0] == cuts, device[1] == dom)

        @pl.when(self_target)
        def _():
            pltpu.make_async_copy(src, dst, rsem).start()

        @pl.when(jnp.logical_not(self_target))
        def _():
            remote(src, dst, ssem, rsem, device).start()

    def sent(src, dst, ssem, rsem, device):
        self_target = jnp.logical_and(device[0] == cuts, device[1] == dom)

        @pl.when(jnp.logical_not(self_target))
        def _():
            remote(src, dst, ssem, rsem, device).wait_send()

    def received(dst, rsem):
        pltpu.make_async_copy(dst, dst, rsem).wait()

    greeted = peers[1:]
    for a in range(2):
        greeted.append(role_device(2 * cuts + a, x_hi, u, core))
        greeted.append(role_device(2 * cuts + a, x_hi, u, 1 - core))
        greeted.append(home_device(number, w, a, u, core))
        greeted.append(home_device(number, w, a, u, 1 - core))
        for moved, end in ((ITERS - 1, last_number), (ITERS, row_number)):
            greeted.append(home_device(end, w, a, u, core))
            greeted.append(role_device((2 * cuts + a + SLICES - moved) % SLICES, x_hi, u, core))
    greeted.append(ahead)
    greeted.append(role_device((number + 1) % SLICES, w, u, core))
    barrier = pltpu.get_barrier_semaphore()
    expected = 0
    for device in greeted:
        others = jnp.logical_or(device[0] != cuts, device[1] != dom)
        expected = expected + others.astype(jnp.int32)

        @pl.when(others)
        def _():
            pl.semaphore_signal(barrier, inc=1, device_id=device, device_id_type=MESH)

    loads = [
        pltpu.make_async_copy(src, dst, in_sem.at[index])
        for index, (src, dst) in enumerate(
            [
                (radiation_hbm, radiation),
                (electrons_hbm, electrons),
                (cell_index_hbm, cell_index),
                (cell_offset_hbm, cell_offset),
                (kx_hbm, kx),
                (ky_hbm, ky),
            ]
        )
    ]
    for load in loads:
        load.start()
    for load in loads[0:4]:
        load.wait()
    for p in range(2):
        for half in range(2):
            for part in range(2):
                column = part * 256 + half * 128
                rad[p, half, :, part * 128 : part * 128 + 128] = radiation[
                    :, p, column : column + 128
                ]
        for row in range(ROWS):
            lanes = slice(row * LANES, row * LANES + LANES)
            for field_number in range(2):
                place = slice(row, row + 1)
                el_in[p, field_number, place] = electrons[field_number, p : p + 1, lanes]
                el_in[p, 2 + field_number, place] = cell_index[
                    field_number, p : p + 1, lanes
                ].astype(f32)
                el_in[p, 4 + field_number, place] = cell_offset[field_number, p : p + 1, lanes]
    pl.semaphore_wait(barrier, expected)

    own_slot = y_hi * 2 + core
    starts = []
    for p in range(2):
        starts.append(
            (
                rad.at[p],
                p_send.at[:, y_hi],
                row_send.at[p],
                row_sem.at[y_hi],
                role_device(2 * cuts + p, x_hi, u, core),
            )
        )
    for p in range(2):
        for number_core in range(2):
            starts.append(
                (
                    el_in.at[p],
                    el.at[0, own_slot],
                    init_send.at[p, number_core],
                    el_sem.at[own_slot],
                    role_device(2 * cuts + p, x_hi, u, (core + number_core) % 2),
                )
            )
    for args in starts:
        send(*args)

    for load in loads[4:6]:
        load.wait()
    kr, ki = kx[0], kx[1]
    for number_part, part in enumerate(split(jnp.concatenate([kr, ki], axis=1))):
        k2[number_part * 256 : number_part * 256 + 256] = part
    for half_in in range(2):
        for half_out in range(2):
            block_re = ky[0, half_in * 128 : half_in * 128 + 128, half_out * 128 : half_out * 128 + 128]
            block_im = ky[1, half_in * 128 : half_in * 128 + 128, half_out * 128 : half_out * 128 + 128]
            rows = jnp.concatenate(
                [
                    jnp.concatenate([block_re, block_im], axis=1),
                    jnp.concatenate([-block_im, block_re], axis=1),
                ],
                axis=0,
            )
            for number_part, part in enumerate(split(rows)):
                big_y[
                    number_part,
                    half_in * 256 : half_in * 256 + 256,
                    half_out * 256 : half_out * 256 + 256,
                ] = part

    def gather_copy(step):
        return remote(
            p_send.at[(core + step) % 2],
            field.at[q],
            ag_send.at[step],
            ag_sem.at[step],
            peers[step],
        )

    def sums_copy(step):
        return remote(
            mixed.at[owners[step]], sums.at[q], rs_send.at[step], rs_sem.at[step], peers[step]
        )

    def start_gather():
        for step in SEND_ORDER:
            gather_copy(step).start()
        field[q] = p_send[core]

    def a_copy(block):
        return remote(
            a_send.at[block], a_recv.at[block], a_ssem.at[block], a_rsem.at[block], beside
        )

    def place_copy(n):
        return remote(
            el.at[n, :, 2:6], el.at[n + 1, :, 2:6], place_send.at[n], place_sem.at[n], ahead
        )

    def state_copy(n, block):
        return remote(
            el.at[n, block, 0:2],
            el.at[n + 1, block, 0:2],
            state_send.at[n, block],
            state_sem.at[n, block],
            ahead,
        )

    def out_electrons(part):
        return (
            el_send.at[part],
            el_back.at[last_number % 2],
            out_send.at[2 + part],
            out_sem.at[2 + last_number % 2],
            home_device(last_number, w, part, u, core),
        )

    def out_rows(part):
        return (
            p_out.at[part],
            rad_back.at[row_number % 2],
            out_send.at[part],
            out_sem.at[row_number % 2],
            home_device(row_number, w, part, u, core),
        )

    def build(n, first):
        @pl.loop(0, BLOCKS)
        def _(block):
            if first:
                received(el.at[0, block], el_sem.at[block])
            grid_x = lax.broadcasted_iota(jnp.int32, (256, LANES), 0).astype(f32).astype(bf16)
            grid_y = (lax.broadcasted_iota(jnp.int32, (128, LANES), 0) + core * 128).astype(f32)
            none = jnp.zeros((256, LANES), bf16)
            for row in range(ROWS):
                index_x = el[n, block, 2, row : row + 1, :]
                index_y = el[n, block, 3, row : row + 1, :]
                offset_x = el[n, block, 4, row : row + 1, :]
                offset_y = el[n, block, 5, row : row + 1, :]
                lanes = slice(row * LANES, row * LANES + LANES)
                lower, lower_low = split(1.0 - offset_x, LOW)
                upper, upper_low = split(offset_x, LOW)
                at_lower = grid_x == index_x.astype(bf16)
                at_upper = grid_x == (index_x + 1.0).astype(bf16)
                hi = jnp.where(at_lower, lower, jnp.where(at_upper, upper, none))
                lo = jnp.where(at_lower, lower_low, jnp.where(at_upper, upper_low, none))
                wx[block, 0:256, lanes] = hi
                w8[block, 0:256, lanes] = hi.astype(f8)
                w8[block, 256:512, lanes] = lo.astype(f8)
                wy[block, :, lanes] = jnp.where(
                    grid_y == index_y,
                    1.0 - offset_y,
                    jnp.where(grid_y == index_y + 1.0, offset_y, 0.0),
                )
            trig[block, 0] = jnp.cos(el[n, block, 0])
            trig[block, 1] = jnp.sin(el[n, block, 0])

    def advance(n, last):
        if not last:
            place_copy(n).start()
        for step in SEND_ORDER:
            received(field.at[owners[step]], ag_sem.at[step])
        full = jnp.concatenate([field[owner, part] for owner, part in ROW_BLOCKS], axis=0)
        turned = full.T
        peak = jnp.max(jnp.max(jnp.abs(turned), axis=0, keepdims=True), axis=1, keepdims=True)
        peak = jnp.maximum(peak, 1e-30)
        scaled = turned * (PEAK / peak)
        hi, lo = split_low(scaled)
        low = jnp.concatenate([lo, scaled.astype(f8)], axis=1)
        unscale = jnp.broadcast_to(peak * (1.0 / PEAK), (1, LANES))

        @pl.loop(0, BLOCKS)
        def _(block):
            for row in range(ROWS):
                lanes = slice(row * LANES, row * LANES + LANES)
                values = mm(hi, wx[block, :, lanes]) + mm(low, w8[block, :, lanes]) * (1.0 / LOW)
                weight = wy[block, :, lanes]
                a_send[block, 0, row : row + 1, :] = unscale * jnp.sum(
                    values[0:128] * weight, axis=0, keepdims=True
                )
                a_send[block, 1, row : row + 1, :] = unscale * jnp.sum(
                    values[128:256] * weight, axis=0, keepdims=True
                )
            a_copy(block).start()

        current[...] = 0.25 * full

        @pl.loop(0, BLOCKS)
        def _(block):
            received(a_recv.at[block], a_rsem.at[block])
            a_re = a_send[block, 0] + a_recv[block, 0]
            a_im = a_send[block, 1] + a_recv[block, 1]
            energy = el[n, block, 1] - coupling * (a_re * trig[block, 0] - a_im * trig[block, 1])
            phase = el[n, block, 0] + phase_step * energy
            el[n, block, 0] = phase
            el[n, block, 1] = energy
            if not last:
                state_copy(n, block).start()
            cos, sin = jnp.cos(phase), jnp.sin(phase)
            for row in range(ROWS):
                lanes = slice(row * LANES, row * LANES + LANES)
                weight = current_gain * wy[block, :, lanes]
                values = jnp.concatenate(
                    [weight * cos[row : row + 1, :], -weight * sin[row : row + 1, :]], axis=0
                )
                hi, lo = split_low(values)
                v_hi[:, lanes] = hi
                v_lo[:, lanes] = lo
                v_top[:, lanes] = values.astype(f8)
            current[...] += mm_nt(wx[block], v_hi[...]) + (
                mm_nt(w8[block, 0:256], v_lo[...]) + mm_nt(w8[block, 256:512], v_top[...])
            ) * (1.0 / LOW)

        if last:
            for part in range(2):
                el_send[part] = el[n, part * 2 + core, 0:2]
                send(*out_electrons(part))

        total = current[...]
        re, im = total[:, 0:128], total[:, 128:256]
        stacked = jnp.concatenate([total, jnp.concatenate([-im, re], axis=1)], axis=0)
        hi, lo = split(stacked)
        product = mm(k2[...], hi)
        product = product[0:256] + product[256:512] + mm(k2[0:256], lo)
        for index, (owner, part) in enumerate(ROW_BLOCKS):
            mixed[owner, part] = product[index * 16 : index * 16 + 16]
        for step in SEND_ORDER:
            sums_copy(step).start()
        sums[q] = mixed[q]
        for step in SEND_ORDER:
            gather_copy(step).wait_send()
        if not last:
            received(el.at[n + 1, :, 2:6], place_sem.at[n])

            @pl.loop(0, BLOCKS)
            def _(block):
                received(el.at[n + 1, block, 0:2], state_sem.at[n, block])

            build(n + 1, False)
        for step in SEND_ORDER:
            received(sums.at[owners[step]], rs_sem.at[step])
        halves = [
            ((sums[half] + sums[half + 2]) + (sums[half + 4] + sums[half + 6])).reshape(32, 256)
            for half in range(2)
        ]
        hi, lo = split(jnp.concatenate(halves, axis=1))
        result = mm(jnp.concatenate([hi, lo], axis=0), big_y[0])
        result = result[0:32] + result[32:64] + mm(hi, big_y[1])
        result = jnp.where((number + n + 1) % SLICES == 0, 0.0, result)
        if last:
            p_out[...] = jnp.concatenate(
                [result[:, 0:128], result[:, 256:384], result[:, 128:256], result[:, 384:512]],
                axis=1,
            ).reshape(p_out.shape)
            for part in range(2):
                send(*out_rows(part))
        else:
            for half in range(2):
                p_send[half] = result[:, half * 256 : half * 256 + 256].reshape(2, 16, 256)
            start_gather()
            place_copy(n).wait_send()

        for step in SEND_ORDER:
            sums_copy(step).wait_send()
        for block in range(BLOCKS):
            a_copy(block).wait_send()
            if not last:
                state_copy(n, block).wait_send()

    for part in range(2):
        received(p_send.at[:, part], row_sem.at[part])
    start_gather()
    build(0, True)

    @pl.loop(0, ITERS - 1)
    def _(n):
        advance(n, False)

    advance(ITERS - 1, True)

    for args in starts:
        sent(*args)
    for part in range(2):
        sent(*out_rows(part))
        sent(*out_electrons(part))
    for part in range(2):
        received(rad_back.at[part], out_sem.at[part])
        received(el_back.at[part], out_sem.at[2 + part])
    for p in range(2):
        radiation_out[:, p, :] = rad_back[p]
        for row in range(ROWS):
            lanes = slice(row * LANES, row * LANES + LANES)
            for field_number in range(2):
                electrons_out[field_number, p : p + 1, lanes] = el_back[
                    p, field_number, row : row + 1
                ]


def shards(radiation, electrons, cell_index, cell_offset, kernel_x, kernel_y):
    vmem = pl.BlockSpec(memory_space=pltpu.VMEM)
    dma = pltpu.SemaphoreType.DMA
    return pl.pallas_call(
        kernel,
        out_shape=(
            jax.ShapeDtypeStruct(radiation.shape, f32),
            jax.ShapeDtypeStruct(electrons.shape, f32),
        ),
        in_specs=[pl.BlockSpec(memory_space=pltpu.HBM)] * 6,
        out_specs=(vmem, vmem),
        scratch_shapes=[
            pltpu.VMEM(radiation.shape, f32),
            pltpu.VMEM(electrons.shape, f32),
            pltpu.VMEM(cell_index.shape, jnp.int32),
            pltpu.VMEM(cell_offset.shape, f32),
            pltpu.VMEM(kernel_x.shape, f32),
            pltpu.VMEM(kernel_y.shape, f32),
            pltpu.VMEM((2, 2, 16, 256), f32),
            pltpu.VMEM((2, 6, ROWS, LANES), f32),
            pltpu.VMEM((2, 16, 512), f32),
            pltpu.VMEM((2, 2, ROWS, LANES), f32),
            pltpu.VMEM((ITERS, BLOCKS, 6, ROWS, LANES), f32),
            pltpu.VMEM((BLOCKS, 256, ROWS * LANES), bf16),
            pltpu.VMEM((BLOCKS, 128, ROWS * LANES), f32),
            pltpu.VMEM((8, 2, 16, 256), f32),
            pltpu.VMEM((BLOCKS, 2, ROWS, LANES), f32),
            pltpu.VMEM((BLOCKS, 2, ROWS, LANES), f32),
            pltpu.VMEM((BLOCKS, 2, ROWS, LANES), f32),
            pltpu.VMEM((256, ROWS * LANES), bf16),
            pltpu.VMEM((256, ROWS * LANES), f8),
            pltpu.VMEM((256, ROWS * LANES), f8),
            pltpu.VMEM((BLOCKS, 512, ROWS * LANES), f8),
            pltpu.VMEM((256, 256), f32),
            pltpu.VMEM((512, 512), bf16),
            pltpu.VMEM((2, 512, 512), bf16),
            pltpu.VMEM((8, 2, 16, 256), f32),
            pltpu.VMEM((8, 2, 16, 256), f32),
            pltpu.VMEM((2, 2, 16, 256), f32),
            pltpu.VMEM((2, 16, 512), f32),
            pltpu.VMEM((2, 2, ROWS, LANES), f32),
            dma((2, 2)),
            dma((BLOCKS,)),
            dma((2,)),
            dma((2,)),
            dma((8,)),
            dma((8,)),
            dma((BLOCKS,)),
            dma((BLOCKS,)),
            dma((8,)),
            dma((8,)),
            dma((ITERS,)),
            dma((ITERS,)),
            dma((ITERS, BLOCKS)),
            dma((ITERS, BLOCKS)),
            dma((4,)),
            dma((4,)),
            dma((6,)),
        ],
        compiler_params=pltpu.CompilerParams(
            collective_id=0, has_side_effects=True, vmem_limit_bytes=63 * 1024 * 1024
        ),
    )(radiation, electrons, cell_index, cell_offset, kernel_x, kernel_y)


def solution(mesh):
    placed = (
        P("dom", "cuts", None),
        P(None, "cuts", "dom"),
        P(None, "cuts", "dom"),
        P(None, "cuts", "dom"),
        P(),
        P(),
    )
    return jax.shard_map(
        shards,
        mesh=mesh,
        in_specs=placed,
        out_specs=(P("dom", "cuts", None), P(None, "cuts", "dom")),
        check_vma=False,
    )
```

```python
import jax
import jax.numpy as jnp
from jax import lax
from jax.experimental import pallas as pl
from jax.experimental.pallas import tpu as pltpu
from jax.sharding import PartitionSpec as P

ITERS = 4
SLICES = 16
coupling = 0.5
phase_step = 1.0
current_gain = 1.0
MESH = pl.DeviceIdType.MESH
f32 = jnp.float32
bf16 = jnp.bfloat16
f8 = jnp.float8_e4m3fn

BLOCKS = 4
ROWS = 8
LANES = 256
SEND_ORDER = (6, 7, 2, 3, 4, 5, 1)
LOW = 4096.0
PEAK = 32.0
ROW_BLOCKS = [
    ((w * 2 + (t + y_lo) % 2) * 2 + core, t)
    for t in range(2)
    for y_lo in range(2)
    for w in range(2)
    for core in range(2)
]


def split(value, scale=1.0):
    hi = value.astype(bf16)
    return hi, ((value - hi.astype(f32)) * scale).astype(bf16)


def split_low(value):
    hi = value.astype(bf16)
    return hi, ((value - hi.astype(f32)) * LOW).astype(f8)


def mm(a, b):
    return jnp.dot(a, b, preferred_element_type=f32)


def mm_nt(a, b):
    return lax.dot_general(a, b, (((1,), (1,)), ((), ())), preferred_element_type=f32)


def role_device(number, w, u, core):
    pair = number // 2
    x_hi, z = pair // 4, pair % 4
    y_hi = (number % 2 + z) % 2
    x_lo, y_lo = (w + x_hi) % 2, (u + y_hi) % 2
    return x_lo * 4 + z, (y_hi * 2 + y_lo) * 4 + x_hi * 2 + core


def home_device(number, w, t, u, core):
    return number // 2, (t * 2 + (u + t) % 2) * 4 + w * 2 + core


def kernel(
    radiation_hbm,
    electrons_hbm,
    cell_index_hbm,
    cell_offset_hbm,
    kx_hbm,
    ky_hbm,
    radiation_out,
    electrons_out,
    radiation,
    electrons,
    cell_index,
    cell_offset,
    kx,
    ky,
    rad,
    el_in,
    rad_back,
    el_back,
    el,
    wx,
    wy,
    field,
    a_send,
    a_recv,
    trig,
    v_hi,
    v_lo,
    v_top,
    w8,
    current,
    k2,
    big_y,
    mixed,
    sums,
    p_send,
    p_out,
    el_send,
    init_send,
    el_sem,
    row_send,
    row_sem,
    ag_send,
    ag_sem,
    a_ssem,
    a_rsem,
    rs_send,
    rs_sem,
    place_send,
    place_sem,
    state_send,
    state_sem,
    out_send,
    out_sem,
    in_sem,
):
    cuts, dom = lax.axis_index("cuts"), lax.axis_index("dom")
    x_lo, z = cuts // 4, cuts % 4
    y, x_hi, core = dom // 4, dom // 2 % 2, dom % 2
    y_hi = y // 2
    w, u = (x_lo + x_hi) % 2, (y + y_hi) % 2
    number = 2 * (x_hi * 4 + z) + (y_hi + z) % 2
    q = (w * 2 + u) * 2 + core
    last_number = (number + ITERS - 1) % SLICES
    row_number = (number + ITERS) % SLICES

    def peer_device(other):
        return role_device(number, other // 4, other // 2 % 2, other % 2)

    owners = [
        ((w + key // 4) % 2 * 2 + (u + key // 2) % 2) * 2 + (core + key) % 2 for key in range(8)
    ]
    peers = [peer_device(owner) for owner in owners]
    beside = peers[1]
    ahead = role_device((number + SLICES - 1) % SLICES, w, u, core)

    def remote(src, dst, ssem, rsem, device):
        return pltpu.make_async_remote_copy(
            src_ref=src,
            dst_ref=dst,
            send_sem=ssem,
            recv_sem=rsem,
            device_id=device,
            device_id_type=MESH,
        )

    def send(src, dst, ssem, rsem, device):
        self_target = jnp.logical_and(device[0] == cuts, device[1] == dom)

        @pl.when(self_target)
        def _():
            pltpu.make_async_copy(src, dst, rsem).start()

        @pl.when(jnp.logical_not(self_target))
        def _():
            remote(src, dst, ssem, rsem, device).start()

    def sent(src, dst, ssem, rsem, device):
        self_target = jnp.logical_and(device[0] == cuts, device[1] == dom)

        @pl.when(jnp.logical_not(self_target))
        def _():
            remote(src, dst, ssem, rsem, device).wait_send()

    def received(dst, rsem):
        pltpu.make_async_copy(dst, dst, rsem).wait()

    greeted = peers[1:]
    for a in range(2):
        greeted.append(role_device(2 * cuts + a, x_hi, u, core))
        greeted.append(role_device(2 * cuts + a, x_hi, u, 1 - core))
        greeted.append(home_device(number, w, a, u, core))
        greeted.append(home_device(number, w, a, u, 1 - core))
        for moved, end in ((ITERS - 1, last_number), (ITERS, row_number)):
            greeted.append(home_device(end, w, a, u, core))
            greeted.append(role_device((2 * cuts + a + SLICES - moved) % SLICES, x_hi, u, core))
    greeted.append(ahead)
    greeted.append(role_device((number + 1) % SLICES, w, u, core))
    barrier = pltpu.get_barrier_semaphore()
    expected = 0
    for device in greeted:
        others = jnp.logical_or(device[0] != cuts, device[1] != dom)
        expected = expected + others.astype(jnp.int32)

        @pl.when(others)
        def _():
            pl.semaphore_signal(barrier, inc=1, device_id=device, device_id_type=MESH)

    loads = [
        pltpu.make_async_copy(src, dst, in_sem.at[index])
        for index, (src, dst) in enumerate(
            [
                (radiation_hbm, radiation),
                (electrons_hbm, electrons),
                (cell_index_hbm, cell_index),
                (cell_offset_hbm, cell_offset),
                (kx_hbm, kx),
                (ky_hbm, ky),
            ]
        )
    ]
    for load in loads:
        load.start()
    for load in loads[0:4]:
        load.wait()
    for p in range(2):
        for half in range(2):
            for part in range(2):
                column = part * 256 + half * 128
                rad[p, half, :, part * 128 : part * 128 + 128] = radiation[
                    :, p, column : column + 128
                ]
        for row in range(ROWS):
            lanes = slice(row * LANES, row * LANES + LANES)
            for field_number in range(2):
                place = slice(row, row + 1)
                el_in[p, field_number, place] = electrons[field_number, p : p + 1, lanes]
                el_in[p, 2 + field_number, place] = cell_index[
                    field_number, p : p + 1, lanes
                ].astype(f32)
                el_in[p, 4 + field_number, place] = cell_offset[field_number, p : p + 1, lanes]
    pl.semaphore_wait(barrier, expected)

    own_slot = y_hi * 2 + core
    starts = []
    for p in range(2):
        starts.append(
            (
                rad.at[p],
                p_send.at[:, y_hi],
                row_send.at[p],
                row_sem.at[y_hi],
                role_device(2 * cuts + p, x_hi, u, core),
            )
        )
    for p in range(2):
        for number_core in range(2):
            starts.append(
                (
                    el_in.at[p],
                    el.at[0, own_slot],
                    init_send.at[p, number_core],
                    el_sem.at[own_slot],
                    role_device(2 * cuts + p, x_hi, u, (core + number_core) % 2),
                )
            )
    for args in starts:
        send(*args)

    for load in loads[4:6]:
        load.wait()
    kr, ki = kx[0], kx[1]
    for number_part, part in enumerate(split(jnp.concatenate([kr, ki], axis=1))):
        k2[number_part * 256 : number_part * 256 + 256] = part
    for half_in in range(2):
        for half_out in range(2):
            block_re = ky[0, half_in * 128 : half_in * 128 + 128, half_out * 128 : half_out * 128 + 128]
            block_im = ky[1, half_in * 128 : half_in * 128 + 128, half_out * 128 : half_out * 128 + 128]
            rows = jnp.concatenate(
                [
                    jnp.concatenate([block_re, block_im], axis=1),
                    jnp.concatenate([-block_im, block_re], axis=1),
                ],
                axis=0,
            )
            for number_part, part in enumerate(split(rows)):
                big_y[
                    number_part,
                    half_in * 256 : half_in * 256 + 256,
                    half_out * 256 : half_out * 256 + 256,
                ] = part

    def gather_copy(step):
        return remote(
            p_send.at[(core + step) % 2],
            field.at[q],
            ag_send.at[step],
            ag_sem.at[step],
            peers[step],
        )

    def sums_copy(step):
        return remote(
            mixed.at[owners[step]], sums.at[q], rs_send.at[step], rs_sem.at[step], peers[step]
        )

    def start_gather():
        for step in SEND_ORDER:
            gather_copy(step).start()
        field[q] = p_send[core]

    def a_copy(block):
        return remote(
            a_send.at[block], a_recv.at[block], a_ssem.at[block], a_rsem.at[block], beside
        )

    def place_copy(n):
        return remote(
            el.at[n, :, 2:6], el.at[n + 1, :, 2:6], place_send.at[n], place_sem.at[n], ahead
        )

    def state_copy(n, block):
        return remote(
            el.at[n, block, 0:2],
            el.at[n + 1, block, 0:2],
            state_send.at[n, block],
            state_sem.at[n, block],
            ahead,
        )

    def out_electrons(part):
        return (
            el_send.at[part],
            el_back.at[last_number % 2],
            out_send.at[2 + part],
            out_sem.at[2 + last_number % 2],
            home_device(last_number, w, part, u, core),
        )

    def out_rows(part):
        return (
            p_out.at[part],
            rad_back.at[row_number % 2],
            out_send.at[part],
            out_sem.at[row_number % 2],
            home_device(row_number, w, part, u, core),
        )

    def build(n, first):
        @pl.loop(0, BLOCKS)
        def _(block):
            if first:
                received(el.at[0, block], el_sem.at[block])
            grid_x = lax.broadcasted_iota(jnp.int32, (256, LANES), 0).astype(f32).astype(bf16)
            grid_y = (lax.broadcasted_iota(jnp.int32, (128, LANES), 0) + core * 128).astype(f32)
            none = jnp.zeros((256, LANES), bf16)
            for row in range(ROWS):
                index_x = el[n, block, 2, row : row + 1, :]
                index_y = el[n, block, 3, row : row + 1, :]
                offset_x = el[n, block, 4, row : row + 1, :]
                offset_y = el[n, block, 5, row : row + 1, :]
                lanes = slice(row * LANES, row * LANES + LANES)
                lower, lower_low = split(1.0 - offset_x, LOW)
                upper, upper_low = split(offset_x, LOW)
                at_lower = grid_x == index_x.astype(bf16)
                at_upper = grid_x == (index_x + 1.0).astype(bf16)
                hi = jnp.where(at_lower, lower, jnp.where(at_upper, upper, none))
                lo = jnp.where(at_lower, lower_low, jnp.where(at_upper, upper_low, none))
                wx[block, 0:256, lanes] = hi
                w8[block, 0:256, lanes] = hi.astype(f8)
                w8[block, 256:512, lanes] = lo.astype(f8)
                wy[block, :, lanes] = jnp.where(
                    grid_y == index_y,
                    1.0 - offset_y,
                    jnp.where(grid_y == index_y + 1.0, offset_y, 0.0),
                )
            trig[block, 0] = jnp.cos(el[n, block, 0])
            trig[block, 1] = jnp.sin(el[n, block, 0])

    def advance(n, last):
        if not last:
            place_copy(n).start()
        for step in SEND_ORDER:
            received(field.at[owners[step]], ag_sem.at[step])
        full = jnp.concatenate([field[owner, part] for owner, part in ROW_BLOCKS], axis=0)
        turned = full.T
        peak = jnp.max(jnp.max(jnp.abs(turned), axis=0, keepdims=True), axis=1, keepdims=True)
        peak = jnp.maximum(peak, 1e-30)
        scaled = turned * (PEAK / peak)
        hi, lo = split_low(scaled)
        low = jnp.concatenate([lo, scaled.astype(f8)], axis=1)
        unscale = jnp.broadcast_to(peak * (1.0 / PEAK), (1, LANES))

        @pl.loop(0, BLOCKS)
        def _(block):
            for row in range(ROWS):
                lanes = slice(row * LANES, row * LANES + LANES)
                values = mm(hi, wx[block, :, lanes]) + mm(low, w8[block, :, lanes]) * (1.0 / LOW)
                weight = wy[block, :, lanes]
                a_send[block, 0, row : row + 1, :] = unscale * jnp.sum(
                    values[0:128] * weight, axis=0, keepdims=True
                )
                a_send[block, 1, row : row + 1, :] = unscale * jnp.sum(
                    values[128:256] * weight, axis=0, keepdims=True
                )
            a_copy(block).start()

        current[...] = 0.25 * full

        @pl.loop(0, BLOCKS)
        def _(block):
            received(a_recv.at[block], a_rsem.at[block])
            a_re = a_send[block, 0] + a_recv[block, 0]
            a_im = a_send[block, 1] + a_recv[block, 1]
            energy = el[n, block, 1] - coupling * (a_re * trig[block, 0] - a_im * trig[block, 1])
            phase = el[n, block, 0] + phase_step * energy
            el[n, block, 0] = phase
            el[n, block, 1] = energy
            if not last:
                state_copy(n, block).start()
            cos, sin = jnp.cos(phase), jnp.sin(phase)
            for row in range(ROWS):
                lanes = slice(row * LANES, row * LANES + LANES)
                weight = current_gain * wy[block, :, lanes]
                values = jnp.concatenate(
                    [weight * cos[row : row + 1, :], -weight * sin[row : row + 1, :]], axis=0
                )
                hi, lo = split_low(values)
                v_hi[:, lanes] = hi
                v_lo[:, lanes] = lo
                v_top[:, lanes] = values.astype(f8)
            current[...] += mm_nt(wx[block], v_hi[...]) + (
                mm_nt(w8[block, 0:256], v_lo[...]) + mm_nt(w8[block, 256:512], v_top[...])
            ) * (1.0 / LOW)

        if last:
            for part in range(2):
                el_send[part] = el[n, part * 2 + core, 0:2]
                send(*out_electrons(part))

        total = current[...]
        re, im = total[:, 0:128], total[:, 128:256]
        stacked = jnp.concatenate([total, jnp.concatenate([-im, re], axis=1)], axis=0)
        hi, lo = split(stacked)
        product = mm(k2[...], hi)
        product = product[0:256] + product[256:512] + mm(k2[0:256], lo)
        for index, (owner, part) in enumerate(ROW_BLOCKS):
            mixed[owner, part] = product[index * 16 : index * 16 + 16]
        for step in SEND_ORDER:
            sums_copy(step).start()
        sums[q] = mixed[q]
        for step in SEND_ORDER:
            gather_copy(step).wait_send()
        if not last:
            received(el.at[n + 1, :, 2:6], place_sem.at[n])

            @pl.loop(0, BLOCKS)
            def _(block):
                received(el.at[n + 1, block, 0:2], state_sem.at[n, block])

            build(n + 1, False)
        for step in SEND_ORDER:
            received(sums.at[owners[step]], rs_sem.at[step])
        halves = [
            ((sums[half] + sums[half + 2]) + (sums[half + 4] + sums[half + 6])).reshape(32, 256)
            for half in range(2)
        ]
        hi, lo = split(jnp.concatenate(halves, axis=1))
        result = mm(jnp.concatenate([hi, lo], axis=0), big_y[0])
        result = result[0:32] + result[32:64] + mm(hi, big_y[1])
        result = jnp.where((number + n + 1) % SLICES == 0, 0.0, result)
        if last:
            p_out[...] = jnp.concatenate(
                [result[:, 0:128], result[:, 256:384], result[:, 128:256], result[:, 384:512]],
                axis=1,
            ).reshape(p_out.shape)
            for part in range(2):
                send(*out_rows(part))
        else:
            for half in range(2):
                p_send[half] = result[:, half * 256 : half * 256 + 256].reshape(2, 16, 256)
            start_gather()
            place_copy(n).wait_send()

        for step in SEND_ORDER:
            sums_copy(step).wait_send()
        for block in range(BLOCKS):
            a_copy(block).wait_send()
            if not last:
                state_copy(n, block).wait_send()

    for part in range(2):
        received(p_send.at[:, part], row_sem.at[part])
    start_gather()
    build(0, True)

    @pl.loop(0, ITERS - 1)
    def _(n):
        advance(n, False)

    advance(ITERS - 1, True)

    for args in starts:
        sent(*args)
    for part in range(2):
        sent(*out_rows(part))
        sent(*out_electrons(part))
    for part in range(2):
        received(rad_back.at[part], out_sem.at[part])
        received(el_back.at[part], out_sem.at[2 + part])
    for p in range(2):
        radiation_out[:, p, :] = rad_back[p]
        for row in range(ROWS):
            lanes = slice(row * LANES, row * LANES + LANES)
            for field_number in range(2):
                electrons_out[field_number, p : p + 1, lanes] = el_back[
                    p, field_number, row : row + 1
                ]


def shards(radiation, electrons, cell_index, cell_offset, kernel_x, kernel_y):
    vmem = pl.BlockSpec(memory_space=pltpu.VMEM)
    dma = pltpu.SemaphoreType.DMA
    return pl.pallas_call(
        kernel,
        out_shape=(
            jax.ShapeDtypeStruct(radiation.shape, f32),
            jax.ShapeDtypeStruct(electrons.shape, f32),
        ),
        in_specs=[pl.BlockSpec(memory_space=pltpu.HBM)] * 6,
        out_specs=(vmem, vmem),
        scratch_shapes=[
            pltpu.VMEM(radiation.shape, f32),
            pltpu.VMEM(electrons.shape, f32),
            pltpu.VMEM(cell_index.shape, jnp.int32),
            pltpu.VMEM(cell_offset.shape, f32),
            pltpu.VMEM(kernel_x.shape, f32),
            pltpu.VMEM(kernel_y.shape, f32),
            pltpu.VMEM((2, 2, 16, 256), f32),
            pltpu.VMEM((2, 6, ROWS, LANES), f32),
            pltpu.VMEM((2, 16, 512), f32),
            pltpu.VMEM((2, 2, ROWS, LANES), f32),
            pltpu.VMEM((ITERS, BLOCKS, 6, ROWS, LANES), f32),
            pltpu.VMEM((BLOCKS, 256, ROWS * LANES), bf16),
            pltpu.VMEM((BLOCKS, 128, ROWS * LANES), f32),
            pltpu.VMEM((8, 2, 16, 256), f32),
            pltpu.VMEM((BLOCKS, 2, ROWS, LANES), f32),
            pltpu.VMEM((BLOCKS, 2, ROWS, LANES), f32),
            pltpu.VMEM((BLOCKS, 2, ROWS, LANES), f32),
            pltpu.VMEM((256, ROWS * LANES), bf16),
            pltpu.VMEM((256, ROWS * LANES), f8),
            pltpu.VMEM((256, ROWS * LANES), f8),
            pltpu.VMEM((BLOCKS, 512, ROWS * LANES), f8),
            pltpu.VMEM((256, 256), f32),
            pltpu.VMEM((512, 512), bf16),
            pltpu.VMEM((2, 512, 512), bf16),
            pltpu.VMEM((8, 2, 16, 256), f32),
            pltpu.VMEM((8, 2, 16, 256), f32),
            pltpu.VMEM((2, 2, 16, 256), f32),
            pltpu.VMEM((2, 16, 512), f32),
            pltpu.VMEM((2, 2, ROWS, LANES), f32),
            dma((2, 2)),
            dma((BLOCKS,)),
            dma((2,)),
            dma((2,)),
            dma((8,)),
            dma((8,)),
            dma((BLOCKS,)),
            dma((BLOCKS,)),
            dma((8,)),
            dma((8,)),
            dma((ITERS,)),
            dma((ITERS,)),
            dma((ITERS, BLOCKS)),
            dma((ITERS, BLOCKS)),
            dma((4,)),
            dma((4,)),
            dma((6,)),
        ],
        compiler_params=pltpu.CompilerParams(
            collective_id=0, has_side_effects=True, vmem_limit_bytes=48 * 1024 * 1024
        ),
    )(
        *[
            pltpu.with_memory_space_constraint(array, pltpu.HBM)
            for array in (radiation, electrons, cell_index, cell_offset, kernel_x, kernel_y)
        ]
    )


def solution(mesh):
    placed = (
        P("dom", "cuts", None),
        P(None, "cuts", "dom"),
        P(None, "cuts", "dom"),
        P(None, "cuts", "dom"),
        P(),
        P(),
    )
    return jax.shard_map(
        shards,
        mesh=mesh,
        in_specs=placed,
        out_specs=(P("dom", "cuts", None), P(None, "cuts", "dom")),
        check_vma=False,
    )
```

```python
import jax
import jax.numpy as jnp
from jax import lax
from jax.experimental import pallas as pl
from jax.experimental.pallas import tpu as pltpu
from jax.sharding import PartitionSpec as P

ITERS = 4
SLICES = 16
coupling = 0.5
phase_step = 1.0
current_gain = 1.0
MESH = pl.DeviceIdType.MESH
f32 = jnp.float32
bf16 = jnp.bfloat16
f8 = jnp.float8_e4m3fn

BLOCKS = 4
ROWS = 8
LANES = 256
SEND_ORDER = (6, 7, 2, 3, 4, 5, 1)
LOW = 4096.0
PEAK = 32.0
ROW_BLOCKS = [
    ((w * 2 + (t + y_lo) % 2) * 2 + core, t)
    for t in range(2)
    for y_lo in range(2)
    for w in range(2)
    for core in range(2)
]


def split(value, scale=1.0):
    hi = value.astype(bf16)
    return hi, ((value - hi.astype(f32)) * scale).astype(bf16)


def split_low(value):
    hi = value.astype(bf16)
    return hi, ((value - hi.astype(f32)) * LOW).astype(f8)


def mm(a, b):
    return jnp.dot(a, b, preferred_element_type=f32)


def mm_nt(a, b):
    return lax.dot_general(a, b, (((1,), (1,)), ((), ())), preferred_element_type=f32)


def role_device(number, w, u, core):
    pair = number // 2
    x_hi, z = pair // 4, pair % 4
    y_hi = (number % 2 + z) % 2
    x_lo, y_lo = (w + x_hi) % 2, (u + y_hi) % 2
    return x_lo * 4 + z, (y_hi * 2 + y_lo) * 4 + x_hi * 2 + core


def home_device(number, w, t, u, core):
    return number // 2, (t * 2 + (u + t) % 2) * 4 + w * 2 + core


def kernel(
    radiation_hbm,
    electrons_hbm,
    cell_index_hbm,
    cell_offset_hbm,
    kx_hbm,
    ky_hbm,
    radiation_out,
    electrons_out,
    radiation,
    electrons,
    cell_index,
    cell_offset,
    kx,
    ky,
    rad,
    el_in,
    rad_back,
    el_back,
    el,
    wx,
    wy,
    field,
    a_send,
    a_recv,
    trig,
    v_hi,
    v_lo,
    v_top,
    w8,
    current,
    k2,
    big_y,
    mixed,
    sums,
    p_send,
    p_out,
    el_send,
    init_send,
    el_sem,
    row_send,
    row_sem,
    ag_send,
    ag_sem,
    a_ssem,
    a_rsem,
    rs_send,
    rs_sem,
    place_send,
    place_sem,
    state_send,
    state_sem,
    out_send,
    out_sem,
    in_sem,
):
    cuts, dom = lax.axis_index("cuts"), lax.axis_index("dom")
    x_lo, z = cuts // 4, cuts % 4
    y, x_hi, core = dom // 4, dom // 2 % 2, dom % 2
    y_hi = y // 2
    w, u = (x_lo + x_hi) % 2, (y + y_hi) % 2
    number = 2 * (x_hi * 4 + z) + (y_hi + z) % 2
    q = (w * 2 + u) * 2 + core
    last_number = (number + ITERS - 1) % SLICES
    row_number = (number + ITERS) % SLICES

    def peer_device(other):
        return role_device(number, other // 4, other // 2 % 2, other % 2)

    owners = [
        ((w + key // 4) % 2 * 2 + (u + key // 2) % 2) * 2 + (core + key) % 2 for key in range(8)
    ]
    peers = [peer_device(owner) for owner in owners]
    beside = peers[1]
    ahead = role_device((number + SLICES - 1) % SLICES, w, u, core)

    def remote(src, dst, ssem, rsem, device):
        return pltpu.make_async_remote_copy(
            src_ref=src,
            dst_ref=dst,
            send_sem=ssem,
            recv_sem=rsem,
            device_id=device,
            device_id_type=MESH,
        )

    def send(src, dst, ssem, rsem, device):
        self_target = jnp.logical_and(device[0] == cuts, device[1] == dom)

        @pl.when(self_target)
        def _():
            pltpu.make_async_copy(src, dst, rsem).start()

        @pl.when(jnp.logical_not(self_target))
        def _():
            remote(src, dst, ssem, rsem, device).start()

    def sent(src, dst, ssem, rsem, device):
        self_target = jnp.logical_and(device[0] == cuts, device[1] == dom)

        @pl.when(jnp.logical_not(self_target))
        def _():
            remote(src, dst, ssem, rsem, device).wait_send()

    def received(dst, rsem):
        pltpu.make_async_copy(dst, dst, rsem).wait()

    greeted = peers[1:]
    for a in range(2):
        greeted.append(role_device(2 * cuts + a, x_hi, u, core))
        greeted.append(role_device(2 * cuts + a, x_hi, u, 1 - core))
        greeted.append(home_device(number, w, a, u, core))
        greeted.append(home_device(number, w, a, u, 1 - core))
        for moved, end in ((ITERS - 1, last_number), (ITERS, row_number)):
            greeted.append(home_device(end, w, a, u, core))
            greeted.append(role_device((2 * cuts + a + SLICES - moved) % SLICES, x_hi, u, core))
    greeted.append(ahead)
    greeted.append(role_device((number + 1) % SLICES, w, u, core))
    barrier = pltpu.get_barrier_semaphore()
    expected = 0
    for device in greeted:
        others = jnp.logical_or(device[0] != cuts, device[1] != dom)
        expected = expected + others.astype(jnp.int32)

        @pl.when(others)
        def _():
            pl.semaphore_signal(barrier, inc=1, device_id=device, device_id_type=MESH)

    loads = [
        pltpu.make_async_copy(src, dst, in_sem.at[index])
        for index, (src, dst) in enumerate(
            [
                (radiation_hbm, radiation),
                (electrons_hbm, electrons),
                (cell_index_hbm, cell_index),
                (cell_offset_hbm, cell_offset),
                (kx_hbm, kx),
                (ky_hbm, ky),
            ]
        )
    ]
    for load in loads:
        load.start()
    loads[0].wait()
    for p in range(2):
        for half in range(2):
            for part in range(2):
                column = part * 256 + half * 128
                rad[p, half, :, part * 128 : part * 128 + 128] = radiation[
                    :, p, column : column + 128
                ]
    pl.semaphore_wait(barrier, expected)

    own_slot = y_hi * 2 + core
    starts = []
    for p in range(2):
        starts.append(
            (
                rad.at[p],
                p_send.at[:, y_hi],
                row_send.at[p],
                row_sem.at[y_hi],
                role_device(2 * cuts + p, x_hi, u, core),
            )
        )
    for args in starts:
        send(*args)
    for load in loads[1:4]:
        load.wait()
    for p in range(2):
        for row in range(ROWS):
            lanes = slice(row * LANES, row * LANES + LANES)
            for field_number in range(2):
                place = slice(row, row + 1)
                el_in[p, field_number, place] = electrons[field_number, p : p + 1, lanes]
                el_in[p, 2 + field_number, place] = cell_index[
                    field_number, p : p + 1, lanes
                ].astype(f32)
                el_in[p, 4 + field_number, place] = cell_offset[field_number, p : p + 1, lanes]
    for p in range(2):
        for number_core in range(2):
            starts.append(
                (
                    el_in.at[p],
                    el.at[0, own_slot],
                    init_send.at[p, number_core],
                    el_sem.at[own_slot],
                    role_device(2 * cuts + p, x_hi, u, (core + number_core) % 2),
                )
            )
    for args in starts[2:]:
        send(*args)

    for load in loads[4:6]:
        load.wait()
    kr, ki = kx[0], kx[1]
    for number_part, part in enumerate(split(jnp.concatenate([kr, ki], axis=1))):
        k2[number_part * 256 : number_part * 256 + 256] = part
    for half_in in range(2):
        for half_out in range(2):
            block_re = ky[0, half_in * 128 : half_in * 128 + 128, half_out * 128 : half_out * 128 + 128]
            block_im = ky[1, half_in * 128 : half_in * 128 + 128, half_out * 128 : half_out * 128 + 128]
            rows = jnp.concatenate(
                [
                    jnp.concatenate([block_re, block_im], axis=1),
                    jnp.concatenate([-block_im, block_re], axis=1),
                ],
                axis=0,
            )
            for number_part, part in enumerate(split(rows)):
                big_y[
                    number_part,
                    half_in * 256 : half_in * 256 + 256,
                    half_out * 256 : half_out * 256 + 256,
                ] = part

    def gather_copy(step):
        return remote(
            p_send.at[(core + step) % 2],
            field.at[q],
            ag_send.at[step],
            ag_sem.at[step],
            peers[step],
        )

    def sums_copy(step):
        return remote(
            mixed.at[owners[step]], sums.at[q], rs_send.at[step], rs_sem.at[step], peers[step]
        )

    def start_gather():
        for step in SEND_ORDER:
            gather_copy(step).start()
        field[q] = p_send[core]

    def a_copy(block):
        return remote(
            a_send.at[block], a_recv.at[block], a_ssem.at[block], a_rsem.at[block], beside
        )

    def place_copy(n):
        return remote(
            el.at[n, :, 2:6], el.at[n + 1, :, 2:6], place_send.at[n], place_sem.at[n], ahead
        )

    def state_copy(n, block):
        return remote(
            el.at[n, block, 0:2],
            el.at[n + 1, block, 0:2],
            state_send.at[n, block],
            state_sem.at[n, block],
            ahead,
        )

    def out_electrons(part):
        return (
            el_send.at[part],
            el_back.at[last_number % 2],
            out_send.at[2 + part],
            out_sem.at[2 + last_number % 2],
            home_device(last_number, w, part, u, core),
        )

    def out_rows(part):
        return (
            p_out.at[part],
            rad_back.at[row_number % 2],
            out_send.at[part],
            out_sem.at[row_number % 2],
            home_device(row_number, w, part, u, core),
        )

    def build(n, first):
        @pl.loop(0, BLOCKS)
        def _(block):
            if first:
                received(el.at[0, block], el_sem.at[block])
            grid_x = lax.broadcasted_iota(jnp.int32, (256, LANES), 0).astype(f32).astype(bf16)
            grid_y = (lax.broadcasted_iota(jnp.int32, (128, LANES), 0) + core * 128).astype(f32)
            none = jnp.zeros((256, LANES), bf16)
            for row in range(ROWS):
                index_x = el[n, block, 2, row : row + 1, :]
                index_y = el[n, block, 3, row : row + 1, :]
                offset_x = el[n, block, 4, row : row + 1, :]
                offset_y = el[n, block, 5, row : row + 1, :]
                lanes = slice(row * LANES, row * LANES + LANES)
                lower, lower_low = split(1.0 - offset_x, LOW)
                upper, upper_low = split(offset_x, LOW)
                at_lower = grid_x == index_x.astype(bf16)
                at_upper = grid_x == (index_x + 1.0).astype(bf16)
                hi = jnp.where(at_lower, lower, jnp.where(at_upper, upper, none))
                lo = jnp.where(at_lower, lower_low, jnp.where(at_upper, upper_low, none))
                wx[block, 0:256, lanes] = hi
                w8[block, 0:256, lanes] = hi.astype(f8)
                w8[block, 256:512, lanes] = lo.astype(f8)
                wy[block, :, lanes] = jnp.where(
                    grid_y == index_y,
                    1.0 - offset_y,
                    jnp.where(grid_y == index_y + 1.0, offset_y, 0.0),
                )
            trig[block, 0] = jnp.cos(el[n, block, 0])
            trig[block, 1] = jnp.sin(el[n, block, 0])

    def advance(n):
        moving = n < ITERS - 1

        @pl.when(moving)
        def _():
            place_copy(n).start()

        for step in SEND_ORDER:
            received(field.at[owners[step]], ag_sem.at[step])
        full = jnp.concatenate([field[owner, part] for owner, part in ROW_BLOCKS], axis=0)
        turned = full.T
        peak = jnp.max(jnp.max(jnp.abs(turned), axis=0, keepdims=True), axis=1, keepdims=True)
        peak = jnp.maximum(peak, 1e-30)
        scaled = turned * (PEAK / peak)
        hi, lo = split_low(scaled)
        hi = (hi.astype(f32) * LOW).astype(bf16)
        low = jnp.concatenate([lo, scaled.astype(f8)], axis=1)
        unscale = jnp.broadcast_to(peak * (1.0 / (PEAK * LOW)), (1, LANES))

        @pl.loop(0, BLOCKS)
        def _(block):
            for row in range(ROWS):
                lanes = slice(row * LANES, row * LANES + LANES)
                values = mm(hi, wx[block, :, lanes]) + mm(low, w8[block, :, lanes])
                weight = wy[block, :, lanes]
                a_send[block, 0, row : row + 1, :] = unscale * jnp.sum(
                    values[0:128] * weight, axis=0, keepdims=True
                )
                a_send[block, 1, row : row + 1, :] = unscale * jnp.sum(
                    values[128:256] * weight, axis=0, keepdims=True
                )
            a_copy(block).start()

        current[...] = 0.25 * full

        @pl.loop(0, BLOCKS)
        def _(block):
            received(a_recv.at[block], a_rsem.at[block])
            a_re = a_send[block, 0] + a_recv[block, 0]
            a_im = a_send[block, 1] + a_recv[block, 1]
            energy = el[n, block, 1] - coupling * (a_re * trig[block, 0] - a_im * trig[block, 1])
            phase = el[n, block, 0] + phase_step * energy
            el[n, block, 0] = phase
            el[n, block, 1] = energy

            @pl.when(moving)
            def _():
                state_copy(n, block).start()

            cos, sin = jnp.cos(phase), jnp.sin(phase)
            for row in range(ROWS):
                lanes = slice(row * LANES, row * LANES + LANES)
                weight = current_gain * wy[block, :, lanes]
                values = jnp.concatenate(
                    [weight * cos[row : row + 1, :], -weight * sin[row : row + 1, :]], axis=0
                )
                hi, lo = split_low(values)
                v_hi[:, lanes] = hi
                v_lo[:, lanes] = lo
                v_top[:, lanes] = values.astype(f8)
            current[...] += mm_nt(wx[block], v_hi[...]) + (
                mm_nt(w8[block, 0:256], v_lo[...]) + mm_nt(w8[block, 256:512], v_top[...])
            ) * (1.0 / LOW)

        @pl.when(jnp.logical_not(moving))
        def _():
            for part in range(2):
                el_send[part] = el[n, part * 2 + core, 0:2]
                send(*out_electrons(part))

        total = current[...]
        re, im = total[:, 0:128], total[:, 128:256]
        stacked = jnp.concatenate([total, jnp.concatenate([-im, re], axis=1)], axis=0)
        hi, lo = split(stacked)
        product = mm(k2[...], hi)
        product = product[0:256] + product[256:512] + mm(k2[0:256], lo)
        for index, (owner, part) in enumerate(ROW_BLOCKS):
            mixed[owner, part] = product[index * 16 : index * 16 + 16]
        for step in SEND_ORDER:
            sums_copy(step).start()
        sums[q] = mixed[q]
        for step in SEND_ORDER:
            gather_copy(step).wait_send()
        @pl.when(moving)
        def _():
            received(el.at[n + 1, :, 2:6], place_sem.at[n])

            @pl.loop(0, BLOCKS)
            def _(block):
                received(el.at[n + 1, block, 0:2], state_sem.at[n, block])

            build(n + 1, False)
        for step in SEND_ORDER:
            received(sums.at[owners[step]], rs_sem.at[step])
        halves = [
            ((sums[half] + sums[half + 2]) + (sums[half + 4] + sums[half + 6])).reshape(32, 256)
            for half in range(2)
        ]
        hi, lo = split(jnp.concatenate(halves, axis=1))
        result = mm(jnp.concatenate([hi, lo], axis=0), big_y[0])
        result = result[0:32] + result[32:64] + mm(hi, big_y[1])
        result = jnp.where((number + n + 1) % SLICES == 0, 0.0, result)
        @pl.when(jnp.logical_not(moving))
        def _():
            p_out[...] = jnp.concatenate(
                [result[:, 0:128], result[:, 256:384], result[:, 128:256], result[:, 384:512]],
                axis=1,
            ).reshape(p_out.shape)
            for part in range(2):
                send(*out_rows(part))
        @pl.when(moving)
        def _():
            for half in range(2):
                p_send[half] = result[:, half * 256 : half * 256 + 256].reshape(2, 16, 256)
            start_gather()
            place_copy(n).wait_send()

        for step in SEND_ORDER:
            sums_copy(step).wait_send()
        for block in range(BLOCKS):
            a_copy(block).wait_send()

            @pl.when(moving)
            def _():
                state_copy(n, block).wait_send()

    for part in range(2):
        received(p_send.at[:, part], row_sem.at[part])
    start_gather()
    build(0, True)

    @pl.loop(0, ITERS)
    def _(n):
        advance(n)

    for args in starts:
        sent(*args)
    for part in range(2):
        sent(*out_rows(part))
        sent(*out_electrons(part))
    for part in range(2):
        received(rad_back.at[part], out_sem.at[part])
        received(el_back.at[part], out_sem.at[2 + part])
    for p in range(2):
        radiation_out[:, p, :] = rad_back[p]
        for row in range(ROWS):
            lanes = slice(row * LANES, row * LANES + LANES)
            for field_number in range(2):
                electrons_out[field_number, p : p + 1, lanes] = el_back[
                    p, field_number, row : row + 1
                ]


def shards(radiation, electrons, cell_index, cell_offset, kernel_x, kernel_y):
    vmem = pl.BlockSpec(memory_space=pltpu.VMEM)
    dma = pltpu.SemaphoreType.DMA
    return pl.pallas_call(
        kernel,
        out_shape=(
            jax.ShapeDtypeStruct(radiation.shape, f32),
            jax.ShapeDtypeStruct(electrons.shape, f32),
        ),
        in_specs=[pl.BlockSpec(memory_space=pltpu.HBM)] * 6,
        out_specs=(vmem, vmem),
        scratch_shapes=[
            pltpu.VMEM(radiation.shape, f32),
            pltpu.VMEM(electrons.shape, f32),
            pltpu.VMEM(cell_index.shape, jnp.int32),
            pltpu.VMEM(cell_offset.shape, f32),
            pltpu.VMEM(kernel_x.shape, f32),
            pltpu.VMEM(kernel_y.shape, f32),
            pltpu.VMEM((2, 2, 16, 256), f32),
            pltpu.VMEM((2, 6, ROWS, LANES), f32),
            pltpu.VMEM((2, 16, 512), f32),
            pltpu.VMEM((2, 2, ROWS, LANES), f32),
            pltpu.VMEM((ITERS, BLOCKS, 6, ROWS, LANES), f32),
            pltpu.VMEM((BLOCKS, 256, ROWS * LANES), bf16),
            pltpu.VMEM((BLOCKS, 128, ROWS * LANES), f32),
            pltpu.VMEM((8, 2, 16, 256), f32),
            pltpu.VMEM((BLOCKS, 2, ROWS, LANES), f32),
            pltpu.VMEM((BLOCKS, 2, ROWS, LANES), f32),
            pltpu.VMEM((BLOCKS, 2, ROWS, LANES), f32),
            pltpu.VMEM((256, ROWS * LANES), bf16),
            pltpu.VMEM((256, ROWS * LANES), f8),
            pltpu.VMEM((256, ROWS * LANES), f8),
            pltpu.VMEM((BLOCKS, 512, ROWS * LANES), f8),
            pltpu.VMEM((256, 256), f32),
            pltpu.VMEM((512, 512), bf16),
            pltpu.VMEM((2, 512, 512), bf16),
            pltpu.VMEM((8, 2, 16, 256), f32),
            pltpu.VMEM((8, 2, 16, 256), f32),
            pltpu.VMEM((2, 2, 16, 256), f32),
            pltpu.VMEM((2, 16, 512), f32),
            pltpu.VMEM((2, 2, ROWS, LANES), f32),
            dma((2, 2)),
            dma((BLOCKS,)),
            dma((2,)),
            dma((2,)),
            dma((8,)),
            dma((8,)),
            dma((BLOCKS,)),
            dma((BLOCKS,)),
            dma((8,)),
            dma((8,)),
            dma((ITERS,)),
            dma((ITERS,)),
            dma((ITERS, BLOCKS)),
            dma((ITERS, BLOCKS)),
            dma((4,)),
            dma((4,)),
            dma((6,)),
        ],
        compiler_params=pltpu.CompilerParams(
            collective_id=0, has_side_effects=True, vmem_limit_bytes=48 * 1024 * 1024
        ),
    )(
        *[
            pltpu.with_memory_space_constraint(array, pltpu.HBM)
            for array in (radiation, electrons, cell_index, cell_offset, kernel_x, kernel_y)
        ]
    )


def solution(mesh):
    placed = (
        P("dom", "cuts", None),
        P(None, "cuts", "dom"),
        P(None, "cuts", "dom"),
        P(None, "cuts", "dom"),
        P(),
        P(),
    )
    return jax.shard_map(
        shards,
        mesh=mesh,
        in_specs=placed,
        out_specs=(P("dom", "cuts", None), P(None, "cuts", "dom")),
        check_vma=False,
    )
```

```python
import jax
import jax.numpy as jnp
from jax import lax
from jax.experimental import pallas as pl
from jax.experimental.pallas import tpu as pltpu
from jax.sharding import PartitionSpec as P

ITERS = 4
SLICES = 16
coupling = 0.5
phase_step = 1.0
current_gain = 1.0
MESH = pl.DeviceIdType.MESH
f32 = jnp.float32
bf16 = jnp.bfloat16
f8 = jnp.float8_e4m3fn

BLOCKS = 4
ROWS = 8
LANES = 256
SEND_ORDER = (6, 7, 2, 3, 4, 5, 1)
LOW = 4096.0
PEAK = 32.0
ROW_BLOCKS = [
    ((w * 2 + (t + y_lo) % 2) * 2 + core, t)
    for t in range(2)
    for y_lo in range(2)
    for w in range(2)
    for core in range(2)
]


def split(value, scale=1.0):
    hi = value.astype(bf16)
    return hi, ((value - hi.astype(f32)) * scale).astype(bf16)


def split_low(value):
    hi = value.astype(bf16)
    return hi, ((value - hi.astype(f32)) * LOW).astype(f8)


def mm(a, b):
    return jnp.dot(a, b, preferred_element_type=f32)


def mm_nt(a, b):
    return lax.dot_general(a, b, (((1,), (1,)), ((), ())), preferred_element_type=f32)


def role_device(number, w, u, core):
    pair = number // 2
    x_hi, z = pair // 4, pair % 4
    y_hi = (number % 2 + z) % 2
    x_lo, y_lo = (w + x_hi) % 2, (u + y_hi) % 2
    return x_lo * 4 + z, (y_hi * 2 + y_lo) * 4 + x_hi * 2 + core


def home_device(number, w, t, u, core):
    return number // 2, (t * 2 + (u + t) % 2) * 4 + w * 2 + core


def kernel(
    radiation_hbm,
    electrons_hbm,
    cell_index_hbm,
    cell_offset_hbm,
    kx_hbm,
    ky_hbm,
    radiation_out,
    electrons_out,
    radiation,
    electrons,
    cell_index,
    cell_offset,
    kx,
    ky,
    rad,
    el_in,
    rad_back,
    el_back,
    el,
    wx,
    wy,
    field,
    a_send,
    a_recv,
    trig,
    v_hi,
    v_lo,
    v_top,
    w8,
    current,
    k2,
    big_y,
    mixed,
    sums,
    p_send,
    p_out,
    el_send,
    init_send,
    el_sem,
    row_send,
    row_sem,
    ag_send,
    ag_sem,
    a_ssem,
    a_rsem,
    rs_send,
    rs_sem,
    place_send,
    place_sem,
    state_send,
    state_sem,
    out_send,
    out_sem,
    in_sem,
):
    cuts, dom = lax.axis_index("cuts"), lax.axis_index("dom")
    x_lo, z = cuts // 4, cuts % 4
    y, x_hi, core = dom // 4, dom // 2 % 2, dom % 2
    y_hi = y // 2
    w, u = (x_lo + x_hi) % 2, (y + y_hi) % 2
    number = 2 * (x_hi * 4 + z) + (y_hi + z) % 2
    q = (w * 2 + u) * 2 + core
    last_number = (number + ITERS - 1) % SLICES
    row_number = (number + ITERS) % SLICES

    def peer_device(other):
        return role_device(number, other // 4, other // 2 % 2, other % 2)

    owners = [
        ((w + key // 4) % 2 * 2 + (u + key // 2) % 2) * 2 + (core + key) % 2 for key in range(8)
    ]
    peers = [peer_device(owner) for owner in owners]
    beside = peers[1]
    ahead = role_device((number + SLICES - 1) % SLICES, w, u, core)

    def remote(src, dst, ssem, rsem, device):
        return pltpu.make_async_remote_copy(
            src_ref=src,
            dst_ref=dst,
            send_sem=ssem,
            recv_sem=rsem,
            device_id=device,
            device_id_type=MESH,
        )

    def send(src, dst, ssem, rsem, device):
        self_target = jnp.logical_and(device[0] == cuts, device[1] == dom)

        @pl.when(self_target)
        def _():
            pltpu.make_async_copy(src, dst, rsem).start()

        @pl.when(jnp.logical_not(self_target))
        def _():
            remote(src, dst, ssem, rsem, device).start()

    def sent(src, dst, ssem, rsem, device):
        self_target = jnp.logical_and(device[0] == cuts, device[1] == dom)

        @pl.when(jnp.logical_not(self_target))
        def _():
            remote(src, dst, ssem, rsem, device).wait_send()

    def received(dst, rsem):
        pltpu.make_async_copy(dst, dst, rsem).wait()

    greeted = peers[1:]
    for a in range(2):
        greeted.append(role_device(2 * cuts + a, x_hi, u, core))
        greeted.append(role_device(2 * cuts + a, x_hi, u, 1 - core))
        greeted.append(home_device(number, w, a, u, core))
        greeted.append(home_device(number, w, a, u, 1 - core))
        for moved, end in ((ITERS - 1, last_number), (ITERS, row_number)):
            greeted.append(home_device(end, w, a, u, core))
            greeted.append(role_device((2 * cuts + a + SLICES - moved) % SLICES, x_hi, u, core))
    greeted.append(ahead)
    greeted.append(role_device((number + 1) % SLICES, w, u, core))
    barrier = pltpu.get_barrier_semaphore()
    expected = 0
    for device in greeted:
        others = jnp.logical_or(device[0] != cuts, device[1] != dom)
        expected = expected + others.astype(jnp.int32)

        @pl.when(others)
        def _():
            pl.semaphore_signal(barrier, inc=1, device_id=device, device_id_type=MESH)

    loads = [
        pltpu.make_async_copy(src, dst, in_sem.at[index])
        for index, (src, dst) in enumerate(
            [
                (radiation_hbm, radiation),
                (electrons_hbm, electrons),
                (cell_index_hbm, cell_index),
                (cell_offset_hbm, cell_offset),
                (kx_hbm, kx),
                (ky_hbm, ky),
            ]
        )
    ]
    for load in loads:
        load.start()
    for load in loads[0:4]:
        load.wait()
    for p in range(2):
        for half in range(2):
            for part in range(2):
                column = part * 256 + half * 128
                rad[p, half, :, part * 128 : part * 128 + 128] = radiation[
                    :, p, column : column + 128
                ]
        for row in range(ROWS):
            lanes = slice(row * LANES, row * LANES + LANES)
            for field_number in range(2):
                place = slice(row, row + 1)
                el_in[p, field_number, place] = electrons[field_number, p : p + 1, lanes]
                el_in[p, 2 + field_number, place] = cell_index[
                    field_number, p : p + 1, lanes
                ].astype(f32)
                el_in[p, 4 + field_number, place] = cell_offset[field_number, p : p + 1, lanes]
    pl.semaphore_wait(barrier, expected)

    own_slot = y_hi * 2 + core
    starts = []
    for p in range(2):
        starts.append(
            (
                rad.at[p],
                p_send.at[:, y_hi],
                row_send.at[p],
                row_sem.at[y_hi],
                role_device(2 * cuts + p, x_hi, u, core),
            )
        )
    for p in range(2):
        for number_core in range(2):
            starts.append(
                (
                    el_in.at[p],
                    el.at[0, own_slot],
                    init_send.at[p, number_core],
                    el_sem.at[own_slot],
                    role_device(2 * cuts + p, x_hi, u, (core + number_core) % 2),
                )
            )
    for args in starts:
        send(*args)

    for load in loads[4:6]:
        load.wait()
    kr, ki = kx[0], kx[1]
    for number_part, part in enumerate(split(jnp.concatenate([kr, ki], axis=1))):
        k2[number_part * 256 : number_part * 256 + 256] = part
    for half_in in range(2):
        for half_out in range(2):
            block_re = ky[0, half_in * 128 : half_in * 128 + 128, half_out * 128 : half_out * 128 + 128]
            block_im = ky[1, half_in * 128 : half_in * 128 + 128, half_out * 128 : half_out * 128 + 128]
            rows = jnp.concatenate(
                [
                    jnp.concatenate([block_re, block_im], axis=1),
                    jnp.concatenate([-block_im, block_re], axis=1),
                ],
                axis=0,
            )
            for number_part, part in enumerate(split(rows)):
                big_y[
                    number_part,
                    half_in * 256 : half_in * 256 + 256,
                    half_out * 256 : half_out * 256 + 256,
                ] = part

    def gather_copy(step):
        return remote(
            p_send.at[(core + step) % 2],
            field.at[q],
            ag_send.at[step],
            ag_sem.at[step],
            peers[step],
        )

    def sums_copy(step):
        return remote(
            mixed.at[owners[step]], sums.at[q], rs_send.at[step], rs_sem.at[step], peers[step]
        )

    def start_gather():
        for step in SEND_ORDER:
            gather_copy(step).start()
        field[q] = p_send[core]

    def a_copy(block):
        return remote(
            a_send.at[block], a_recv.at[block], a_ssem.at[block], a_rsem.at[block], beside
        )

    def place_copy(n):
        return remote(
            el.at[n, :, 2:6], el.at[n + 1, :, 2:6], place_send.at[n], place_sem.at[n], ahead
        )

    def state_copy(n, block):
        return remote(
            el.at[n, block, 0:2],
            el.at[n + 1, block, 0:2],
            state_send.at[n, block],
            state_sem.at[n, block],
            ahead,
        )

    def out_electrons(part):
        return (
            el_send.at[part],
            el_back.at[last_number % 2],
            out_send.at[2 + part],
            out_sem.at[2 + last_number % 2],
            home_device(last_number, w, part, u, core),
        )

    def out_rows(part):
        return (
            p_out.at[part],
            rad_back.at[row_number % 2],
            out_send.at[part],
            out_sem.at[row_number % 2],
            home_device(row_number, w, part, u, core),
        )

    def build(n, first):
        @pl.loop(0, BLOCKS)
        def _(block):
            if first:
                received(el.at[0, block], el_sem.at[block])
            grid_x = lax.broadcasted_iota(jnp.int32, (256, LANES), 0).astype(f32).astype(bf16)
            grid_y = (lax.broadcasted_iota(jnp.int32, (128, LANES), 0) + core * 128).astype(f32)
            none = jnp.zeros((256, LANES), bf16)
            for row in range(ROWS):
                index_x = el[n, block, 2, row : row + 1, :]
                index_y = el[n, block, 3, row : row + 1, :]
                offset_x = el[n, block, 4, row : row + 1, :]
                offset_y = el[n, block, 5, row : row + 1, :]
                lanes = slice(row * LANES, row * LANES + LANES)
                lower, lower_low = split(1.0 - offset_x, LOW)
                upper, upper_low = split(offset_x, LOW)
                at_lower = grid_x == index_x.astype(bf16)
                at_upper = grid_x == (index_x + 1.0).astype(bf16)
                hi = jnp.where(at_lower, lower, jnp.where(at_upper, upper, none))
                lo = jnp.where(at_lower, lower_low, jnp.where(at_upper, upper_low, none))
                wx[block, 0:256, lanes] = hi
                w8[block, 0:256, lanes] = hi.astype(f8)
                w8[block, 256:512, lanes] = lo.astype(f8)
                wy[block, :, lanes] = jnp.where(
                    grid_y == index_y,
                    1.0 - offset_y,
                    jnp.where(grid_y == index_y + 1.0, offset_y, 0.0),
                )
            trig[block, 0] = jnp.cos(el[n, block, 0])
            trig[block, 1] = jnp.sin(el[n, block, 0])

    def advance(n):
        moving = n < ITERS - 1

        @pl.when(moving)
        def _():
            place_copy(n).start()

        for step in SEND_ORDER:
            received(field.at[owners[step]], ag_sem.at[step])
        full = jnp.concatenate([field[owner, part] for owner, part in ROW_BLOCKS], axis=0)
        turned = full.T
        peak = jnp.max(jnp.max(jnp.abs(turned), axis=0, keepdims=True), axis=1, keepdims=True)
        peak = jnp.maximum(peak, 1e-30)
        scaled = turned * (PEAK / peak)
        hi, lo = split_low(scaled)
        low = jnp.concatenate([lo, scaled.astype(f8)], axis=1)
        unscale = jnp.broadcast_to(peak * (1.0 / PEAK), (1, LANES))

        @pl.loop(0, BLOCKS)
        def _(block):
            for row in range(ROWS):
                lanes = slice(row * LANES, row * LANES + LANES)
                values = mm(hi, wx[block, :, lanes]) + mm(low, w8[block, :, lanes]) * (1.0 / LOW)
                weight = wy[block, :, lanes]
                a_send[block, 0, row : row + 1, :] = unscale * jnp.sum(
                    values[0:128] * weight, axis=0, keepdims=True
                )
                a_send[block, 1, row : row + 1, :] = unscale * jnp.sum(
                    values[128:256] * weight, axis=0, keepdims=True
                )
            a_copy(block).start()

        current[...] = 0.25 * full

        @pl.loop(0, BLOCKS)
        def _(block):
            received(a_recv.at[block], a_rsem.at[block])
            a_re = a_send[block, 0] + a_recv[block, 0]
            a_im = a_send[block, 1] + a_recv[block, 1]
            energy = el[n, block, 1] - coupling * (a_re * trig[block, 0] - a_im * trig[block, 1])
            phase = el[n, block, 0] + phase_step * energy
            el[n, block, 0] = phase
            el[n, block, 1] = energy

            @pl.when(moving)
            def _():
                state_copy(n, block).start()

            cos, sin = jnp.cos(phase), jnp.sin(phase)
            for row in range(ROWS):
                lanes = slice(row * LANES, row * LANES + LANES)
                weight = current_gain * wy[block, :, lanes]
                values = jnp.concatenate(
                    [weight * cos[row : row + 1, :], -weight * sin[row : row + 1, :]], axis=0
                )
                hi, lo = split_low(values)
                v_hi[:, lanes] = hi
                v_lo[:, lanes] = lo
                v_top[:, lanes] = values.astype(f8)
            current[...] += mm_nt(wx[block], v_hi[...]) + (
                mm_nt(w8[block, 0:256], v_lo[...]) + mm_nt(w8[block, 256:512], v_top[...])
            ) * (1.0 / LOW)

        @pl.when(jnp.logical_not(moving))
        def _():
            for part in range(2):
                el_send[part] = el[n, part * 2 + core, 0:2]
                send(*out_electrons(part))

        total = current[...]
        re, im = total[:, 0:128], total[:, 128:256]
        stacked = jnp.concatenate([total, jnp.concatenate([-im, re], axis=1)], axis=0)
        hi, lo = split(stacked)
        product = mm(k2[...], hi)
        product = product[0:256] + product[256:512] + mm(k2[0:256], lo)
        for index, (owner, part) in enumerate(ROW_BLOCKS):
            mixed[owner, part] = product[index * 16 : index * 16 + 16]
        for step in SEND_ORDER:
            sums_copy(step).start()
        sums[q] = mixed[q]
        for step in SEND_ORDER:
            gather_copy(step).wait_send()
        @pl.when(moving)
        def _():
            received(el.at[n + 1, :, 2:6], place_sem.at[n])

            @pl.loop(0, BLOCKS)
            def _(block):
                received(el.at[n + 1, block, 0:2], state_sem.at[n, block])

            build(n + 1, False)
        for step in SEND_ORDER:
            received(sums.at[owners[step]], rs_sem.at[step])
        halves = [
            ((sums[half] + sums[half + 2]) + (sums[half + 4] + sums[half + 6])).reshape(32, 256)
            for half in range(2)
        ]
        hi, lo = split(jnp.concatenate(halves, axis=1))
        result = mm(jnp.concatenate([hi, lo], axis=0), big_y[0])
        result = result[0:32] + result[32:64] + mm(hi, big_y[1])
        result = jnp.where((number + n + 1) % SLICES == 0, 0.0, result)
        @pl.when(jnp.logical_not(moving))
        def _():
            p_out[...] = jnp.concatenate(
                [result[:, 0:128], result[:, 256:384], result[:, 128:256], result[:, 384:512]],
                axis=1,
            ).reshape(p_out.shape)
            for part in range(2):
                send(*out_rows(part))
        @pl.when(moving)
        def _():
            for half in range(2):
                p_send[half] = result[:, half * 256 : half * 256 + 256].reshape(2, 16, 256)
            start_gather()
            place_copy(n).wait_send()

        for step in SEND_ORDER:
            sums_copy(step).wait_send()
        for block in range(BLOCKS):
            a_copy(block).wait_send()

            @pl.when(moving)
            def _():
                state_copy(n, block).wait_send()

    for part in range(2):
        received(p_send.at[:, part], row_sem.at[part])
    start_gather()
    build(0, True)

    @pl.loop(0, ITERS)
    def _(n):
        advance(n)

    for args in starts:
        sent(*args)
    for part in range(2):
        sent(*out_rows(part))
        sent(*out_electrons(part))
    for part in range(2):
        received(rad_back.at[part], out_sem.at[part])
        received(el_back.at[part], out_sem.at[2 + part])
    for p in range(2):
        radiation_out[:, p, :] = rad_back[p]
        for row in range(ROWS):
            lanes = slice(row * LANES, row * LANES + LANES)
            for field_number in range(2):
                electrons_out[field_number, p : p + 1, lanes] = el_back[
                    p, field_number, row : row + 1
                ]


def shards(radiation, electrons, cell_index, cell_offset, kernel_x, kernel_y):
    vmem = pl.BlockSpec(memory_space=pltpu.VMEM)
    dma = pltpu.SemaphoreType.DMA
    return pl.pallas_call(
        kernel,
        out_shape=(
            jax.ShapeDtypeStruct(radiation.shape, f32),
            jax.ShapeDtypeStruct(electrons.shape, f32),
        ),
        in_specs=[pl.BlockSpec(memory_space=pltpu.HBM)] * 6,
        out_specs=(vmem, vmem),
        scratch_shapes=[
            pltpu.VMEM(radiation.shape, f32),
            pltpu.VMEM(electrons.shape, f32),
            pltpu.VMEM(cell_index.shape, jnp.int32),
            pltpu.VMEM(cell_offset.shape, f32),
            pltpu.VMEM(kernel_x.shape, f32),
            pltpu.VMEM(kernel_y.shape, f32),
            pltpu.VMEM((2, 2, 16, 256), f32),
            pltpu.VMEM((2, 6, ROWS, LANES), f32),
            pltpu.VMEM((2, 16, 512), f32),
            pltpu.VMEM((2, 2, ROWS, LANES), f32),
            pltpu.VMEM((ITERS, BLOCKS, 6, ROWS, LANES), f32),
            pltpu.VMEM((BLOCKS, 256, ROWS * LANES), bf16),
            pltpu.VMEM((BLOCKS, 128, ROWS * LANES), f32),
            pltpu.VMEM((8, 2, 16, 256), f32),
            pltpu.VMEM((BLOCKS, 2, ROWS, LANES), f32),
            pltpu.VMEM((BLOCKS, 2, ROWS, LANES), f32),
            pltpu.VMEM((BLOCKS, 2, ROWS, LANES), f32),
            pltpu.VMEM((256, ROWS * LANES), bf16),
            pltpu.VMEM((256, ROWS * LANES), f8),
            pltpu.VMEM((256, ROWS * LANES), f8),
            pltpu.VMEM((BLOCKS, 512, ROWS * LANES), f8),
            pltpu.VMEM((256, 256), f32),
            pltpu.VMEM((512, 512), bf16),
            pltpu.VMEM((2, 512, 512), bf16),
            pltpu.VMEM((8, 2, 16, 256), f32),
            pltpu.VMEM((8, 2, 16, 256), f32),
            pltpu.VMEM((2, 2, 16, 256), f32),
            pltpu.VMEM((2, 16, 512), f32),
            pltpu.VMEM((2, 2, ROWS, LANES), f32),
            dma((2, 2)),
            dma((BLOCKS,)),
            dma((2,)),
            dma((2,)),
            dma((8,)),
            dma((8,)),
            dma((BLOCKS,)),
            dma((BLOCKS,)),
            dma((8,)),
            dma((8,)),
            dma((ITERS,)),
            dma((ITERS,)),
            dma((ITERS, BLOCKS)),
            dma((ITERS, BLOCKS)),
            dma((4,)),
            dma((4,)),
            dma((6,)),
        ],
        compiler_params=pltpu.CompilerParams(
            collective_id=0, has_side_effects=True, vmem_limit_bytes=48 * 1024 * 1024
        ),
    )(
        *[
            pltpu.with_memory_space_constraint(array, pltpu.HBM)
            for array in (radiation, electrons, cell_index, cell_offset, kernel_x, kernel_y)
        ]
    )


def solution(mesh):
    placed = (
        P("dom", "cuts", None),
        P(None, "cuts", "dom"),
        P(None, "cuts", "dom"),
        P(None, "cuts", "dom"),
        P(),
        P(),
    )
    return jax.shard_map(
        shards,
        mesh=mesh,
        in_specs=placed,
        out_specs=(P("dom", "cuts", None), P(None, "cuts", "dom")),
        check_vma=False,
    )
```
